512 devices in a mesh: dp: 16 (over z, y_hi), seq: 32 (over y_lo, x, core).
Axes of the slice: x: 4, y: 8 (y_hi: 2, y_lo: 4; y = y_hi * 4 + y_lo), z: 8, core: 2. Of those that a mesh axis runs over, the one named last changes fastest.
Arguments:
- normed: bfloat16 [16, 6144, 2560], P('dp', 'seq'), may hold values from -6 to 6
- values: bfloat16 [16, 6144, 2560], P('dp', 'seq'), may hold values from -6 to 6
- cotangent: bfloat16 [16, 6144, 2560], P('dp', 'seq'), may hold values from -0.59765625 to 0.59765625
- w_bc: bfloat16 [2560, 256], replicated, may hold values from -0.009765625 to 0.009765625
- rate_index: int32 [16, 40, 6144], P('dp', None, 'seq'), may hold values from 0 to 15, as said below
- starts: int32 [16, 6144], P('dp', 'seq'), may hold values 0 or 1
Outputs:
- grad_values: bfloat16 [16, 6144, 2560], P('dp', 'seq')
- grad_wbc: float32 [2560, 256], P(('dp', 'seq'))
The draws below stay inside these ranges and needn't reach their ends.
Inputs may be any that keep to these rules, and one draw needn't show every extreme that they name: `rate_index`: indices into the table of 16 decays.
All inputs are finite; a program needn't handle non-finite values. No bound on the sum of `starts` on one device may be relied on, other than what follows from the above.
Results may differ from the reference program's by a relative error of at most 0.0057.
Values sent between devices are 32-bit elements; how exact they have to be, the bound alone decides.
A program may use at most 64 MiB of HBM per device.

```python
import jax
import jax.numpy as jnp
from jax import lax

D = 2560
H = 40
P_SIZE = 64
N = 128
RATES = 16
TOK_DEV = 192
TOKENS = 6144
PACKS = 16


def draw_rate_index(key, part):
    key_base, key_step = jax.random.split(key)
    start_level = jax.random.randint(key_base, (PACKS, H, 1), 0, RATES - 2)
    region_step = jax.random.randint(key_step, (PACKS, H, TOKENS // TOK_DEV), 0, 3)
    indices = jnp.repeat(region_step, TOK_DEV, axis=2) + start_level
    indices = jnp.minimum(indices, RATES - 1)
    first_level = jnp.where(jnp.arange(H) % 2 == 0, RATES - 1, 0)
    indices = indices.at[:, :, 0].set(jnp.broadcast_to(first_level[None, :], (PACKS, H)))
    return indices.astype(jnp.int32)


def plant(entries, stream_key, low, high):
    longest = entries.shape.index(max(entries.shape))
    spots = []
    for shift in (0, 1):
        where = [jax.random.randint(jax.random.fold_in(stream_key, axis), (), 0, length) for axis, length in enumerate(entries.shape)]
        where[longest] = (where[longest] + shift) % entries.shape[longest]
        spots.append(tuple(where))
    return entries.at[spots[0]].set(low).at[spots[1]].set(high)


def raised(array, own_key, source, target, blocks, factor):
    def block_of(axis_at):
        return (jnp.arange(array.shape[axis_at]) // (array.shape[axis_at] // blocks)).reshape((-1,) + (1,) * (array.ndim - 1 - axis_at))

    first = jax.random.permutation(own_key, blocks)[block_of(target)]
    other_side = (block_of(target) + blocks // 2) % blocks
    return jnp.where((block_of(source) == first) | (block_of(source) == other_side), factor * array, array)


def shard_levels(stream_key, extent, cuts, least, high):
    def one(position, blocks):
        draws = jax.random.uniform(jax.random.fold_in(jax.random.fold_in(stream_key, 6), position), (blocks,), jnp.float32, least / len(cuts), high / len(cuts))
        return jnp.repeat(jnp.exp(draws), extent[position] // blocks).reshape((-1,) + (1,) * (len(extent) - position - 1))

    loudness = one(*cuts[0])
    for cut in cuts[1:]:
        loudness = loudness * one(*cut)
    return loudness


def gaussian(rng, extent, deviation, reach, pieces=(), dtype=jnp.bfloat16):
    entries = jax.random.normal(rng, extent, jnp.float32) * deviation
    if len(pieces) > 0:
        entries = shard_levels(rng, extent, pieces, -0.22, 0.18) * entries
    return jnp.clip(entries, min=-reach, max=reach).astype(dtype)


def bell_draw_with(own_key, extent, scale, bound, cuts, heavy, dtype=jnp.bfloat16):
    entries = scale * jax.random.normal(own_key, extent, jnp.float32)
    if cuts:
        entries = entries * shard_levels(own_key, extent, cuts, -0.22, 0.18)
    return jnp.clip(raised(entries, jax.random.fold_in(own_key, 3), *heavy), -bound, bound).astype(dtype)


def setup_inputs(seed: int = 0) -> dict:
    seeds = jax.random.split(jax.random.key(seed), 7)
    normed = bell_draw_with(seeds[0], (PACKS, TOKENS, D), 1.0, 6.0, ((0, 16), (1, 32)), (1, 2, 32, 2.75))
    values = gaussian(seeds[1], (PACKS, TOKENS, H * P_SIZE), 1.0, 6.0, ((0, 16), (1, 32)))
    cotangent = gaussian(seeds[2], (PACKS, TOKENS, H * P_SIZE), 0.1, 0.59765625, ((0, 16), (1, 32)))
    w_bc = gaussian(seeds[3], (D, 2 * N), (D * N) ** -0.5, 0.009765625)
    rate_index = draw_rate_index(jax.random.fold_in(seeds[6], 71), 0)
    starts = plant((jax.random.randint(seeds[5], (PACKS, TOKENS), 0, 512) < 1).astype(jnp.int32), jax.random.fold_in(seeds[5], 1), 0, 1)
    return dict(normed=normed, values=values, cotangent=cotangent, w_bc=w_bc, rate_index=rate_index, starts=starts)


highest = lax.Precision.HIGHEST
block_len = 64


def rate_logs():
    ranks = jnp.arange(RATES).astype(jnp.float32)
    return -0.0001 * jnp.power(jnp.float32(500.0), ranks / (RATES - 1))


def decay_parts(logrates, flags):
    length = flags.shape[0]
    sums = jnp.cumsum(logrates, axis=1)
    segment = jnp.cumsum(flags.astype(jnp.int32))
    order = jnp.arange(length)
    inside = (segment[:, None] == segment[None, :]) & (order[:, None] >= order[None, :])
    spread = sums[:, :, None] - sums[:, None, :]
    lower_mat = jnp.where(inside[None], jnp.exp(jnp.where(inside[None], spread, 0.0)), 0.0)
    cumulative = jnp.where((segment == 0)[None, :], jnp.exp(sums), 0.0)
    end_weight = lower_mat[:, length - 1, :]
    return lower_mat, cumulative, end_weight


def span_grads(vals, bmat, cmat, cotan, lower_mat, cumulative, end_weight, before, after):
    scores = jnp.dot(cmat, bmat.T, precision=highest)
    mixed = lower_mat * scores[None]
    grad_vals = jnp.einsum('hts,thp->shp', mixed, cotan, precision=highest)
    grad_vals = grad_vals + end_weight.T[:, :, None] * jnp.einsum('sn,hnp->shp', bmat, after, precision=highest)
    paired = lower_mat * jnp.einsum('thp,shp->hts', cotan, vals, precision=highest)
    grad_b = jnp.einsum('hts,tn->sn', paired, cmat, precision=highest)
    grad_b = grad_b + jnp.einsum('hs,shp,hnp->sn', end_weight, vals, after, precision=highest)
    grad_c = jnp.einsum('hts,sn->tn', paired, bmat, precision=highest)
    grad_c = grad_c + jnp.einsum('ht,thp,hnp->tn', cumulative, cotan, before, precision=highest)
    return grad_vals, grad_b, grad_c


def one_pack(items, w_bc):
    normed, values, cotangent, rate_index, starts = items
    tokens = normed.shape[0]
    proj = jnp.dot(normed, w_bc, preferred_element_type=jnp.float32).astype(jnp.bfloat16)
    bmat = proj[:, :N].astype(jnp.float32)
    cmat = proj[:, N:].astype(jnp.float32)
    logrates = rate_logs()[rate_index]
    blocks = tokens // block_len
    vals = values.astype(jnp.float32).reshape(blocks, block_len, H, P_SIZE)
    cots = cotangent.astype(jnp.float32).reshape(blocks, block_len, H, P_SIZE)
    bparts = bmat.reshape(blocks, block_len, N)
    cparts = cmat.reshape(blocks, block_len, N)
    logparts = logrates.reshape(H, blocks, block_len).transpose(1, 0, 2)
    flagparts = starts.reshape(blocks, block_len)
    zero_state = jnp.zeros((H, N, P_SIZE), jnp.float32)

    def forward(carry, piece):
        val, bpart, logpart, flagpart = piece
        lower_mat, cumulative, end_weight = decay_parts(logpart, flagpart)
        ends = jnp.einsum('hk,kn,khp->hnp', end_weight, bpart, val, precision=highest)
        return cumulative[:, -1][:, None, None] * carry + ends, carry

    unused, befores = lax.scan(forward, zero_state, (vals, bparts, logparts, flagparts))

    def backward(carry, piece):
        val, bpart, cpart, cot, logpart, flagpart, before = piece
        lower_mat, cumulative, end_weight = decay_parts(logpart, flagpart)
        grads = span_grads(val, bpart, cpart, cot, lower_mat, cumulative, end_weight, before, carry)
        feeds = jnp.einsum('hk,kn,khp->hnp', cumulative, cpart, cot, precision=highest)
        return feeds + cumulative[:, -1][:, None, None] * carry, grads

    unused_two, (grad_vals, grad_b, grad_c) = lax.scan(backward, zero_state, (vals, bparts, cparts, cots, logparts, flagparts, befores), reverse=True)
    grad_values = grad_vals.reshape(tokens, H * P_SIZE).astype(jnp.bfloat16)
    grad_bc = jnp.concatenate([grad_b.reshape(tokens, N), grad_c.reshape(tokens, N)], axis=1).astype(jnp.bfloat16)
    weight_term = jnp.dot(normed.T, grad_bc, preferred_element_type=jnp.float32)
    return grad_values, weight_term


def reference(normed, values, cotangent, w_bc, rate_index, starts):
    grad_values, terms = lax.map(lambda items: one_pack(items, w_bc), (normed, values, cotangent, rate_index, starts))
    grad_wbc = jnp.sum(terms, axis=0) / (PACKS * TOKENS)
    return grad_values, grad_wbc
```

```python
import jax
import jax.numpy as jnp
from jax import lax
from jax.sharding import PartitionSpec as P

RATES = 16


highest = lax.Precision.HIGHEST


def partner(value, axis, apart):
    mask = 2**apart
    pairs = [(source, source ^ mask) for source in range(lax.axis_size(axis))]
    return lax.ppermute(value, axis, pairs)


def rate_logs():
    ranks = jnp.arange(RATES).astype(jnp.float32)
    return -0.0001 * jnp.power(jnp.float32(500.0), ranks / (RATES - 1))


def decay_parts(logrates, flags):
    length = flags.shape[0]
    sums = jnp.cumsum(logrates, axis=1)
    segment = jnp.cumsum(flags)
    order = jnp.arange(length)
    inside = (segment[:, None] == segment[None, :]) & (order[:, None] >= order[None, :])
    spread = sums[:, :, None] - sums[:, None, :]
    lower_mat = jnp.where(inside[None], jnp.exp(jnp.where(inside[None], spread, 0.0)), 0.0)
    cumulative = jnp.where((segment == 0)[None, :], jnp.exp(sums), 0.0)
    end_weight = lower_mat[:, length - 1, :]
    return (lower_mat, cumulative, end_weight)


def join_pairs(earlier, later):
    return (earlier[0] * later[0], later[0][:, None, None] * earlier[1] + later[1])


def pick_pair(flag, first, second):
    return (jnp.where(flag, first[0], second[0]), jnp.where(flag, first[1], second[1]))


def send_states(pair, bit):
    return partner((pair[0], pair[1]), "seq", bit)


def send_grads(pair, bit):
    return partner((pair[0], pair[1]), "seq", bit)


def combine_chain(own, identity, sender, from_higher):
    position = lax.axis_index("seq")
    levels = lax.axis_size("seq").bit_length() - 1
    prefix = identity
    total = own
    for bit in range(levels):
        other = sender(total, bit)
        high_half = position // (1 << bit) % 2 == 1
        takes_other = jnp.logical_not(high_half) if from_higher else high_half
        prefix = pick_pair(takes_other, join_pairs(other, prefix), prefix)
        total = pick_pair(takes_other, join_pairs(other, total), join_pairs(total, other))
    return prefix


def local(normed, values, cotangent, w_bc, rate_index, starts):
    hidden = normed[0]
    length = hidden.shape[0]
    heads = rate_index.shape[1]
    width = values.shape[2]
    head_dim = width // heads
    state = w_bc.shape[1] // 2
    proj = jnp.dot(hidden, w_bc, preferred_element_type=jnp.float32).astype(jnp.bfloat16)
    bmat = proj[:, :state].astype(jnp.float32)
    cmat = proj[:, state:].astype(jnp.float32)
    levels_table = rate_logs()
    matches = rate_index[0][:, :, None] == jnp.arange(RATES)[None, None, :]
    logrates = jnp.sum(jnp.where(matches, levels_table[None, None, :], 0.0), axis=2)
    lower_mat, cumulative, end_weight = decay_parts(logrates, starts[0])
    vals = values[0].astype(jnp.float32).reshape(length, heads, head_dim)
    cots = cotangent[0].astype(jnp.float32).reshape(length, heads, head_dim)
    decay_total = cumulative[:, -1]
    ends = jnp.einsum("hk,kn,khp->hnp", end_weight, bmat, vals, precision=highest)
    feeds = jnp.einsum("hk,kn,khp->hnp", cumulative, cmat, cots, precision=highest)
    identity = (jnp.ones((heads,), jnp.float32), jnp.zeros((heads, state, head_dim), jnp.float32))
    before = combine_chain((decay_total, ends), identity, send_states, False)[1]
    after = combine_chain((decay_total, feeds), identity, send_grads, True)[1]
    scores = jnp.dot(cmat, bmat.T, precision=highest)
    mixed = lower_mat * scores[None]
    grad_vals = jnp.einsum("hts,thp->shp", mixed, cots, precision=highest)
    grad_vals = grad_vals + end_weight.T[:, :, None] * jnp.einsum(
        "sn,hnp->shp", bmat, after, precision=highest
    )
    paired = lower_mat * jnp.einsum("thp,shp->hts", cots, vals, precision=highest)
    grad_b = jnp.einsum("hts,tn->sn", paired, cmat, precision=highest)
    grad_b = grad_b + jnp.einsum("hs,shp,hnp->sn", end_weight, vals, after, precision=highest)
    grad_c = jnp.einsum("hts,sn->tn", paired, bmat, precision=highest)
    grad_c = grad_c + jnp.einsum("ht,thp,hnp->tn", cumulative, cots, before, precision=highest)
    grad_values = grad_vals.reshape(length, width).astype(jnp.bfloat16)[None]
    grad_bc = jnp.concatenate([grad_b, grad_c], axis=1).astype(jnp.bfloat16)
    scale = 1.0 / (lax.axis_size("dp") * lax.axis_size("seq") * length)
    product = lax.dot_general(
        hidden, grad_bc, (((0,), (0,)), ((), ())), preferred_element_type=jnp.float32
    )
    dp_size, seq_size = lax.axis_size("dp"), lax.axis_size("seq")
    rows, cols = product.shape
    ordered = (product * scale).reshape(dp_size, seq_size, rows // (dp_size * seq_size), cols)
    ordered = ordered.transpose(1, 0, 2, 3).reshape(rows, cols)
    part = lax.psum_scatter(ordered, "seq", scatter_dimension=0, tiled=True)
    grad_wbc = lax.psum_scatter(part, "dp", scatter_dimension=0, tiled=True)
    return (grad_values, grad_wbc)


def solution(mesh):
    placed = (
        P("dp", "seq", None),
        P("dp", "seq", None),
        P("dp", "seq", None),
        P(),
        P("dp", None, "seq"),
        P("dp", "seq"),
    )
    return jax.shard_map(
        local,
        mesh=mesh,
        in_specs=placed,
        out_specs=(P("dp", "seq", None), P(("dp", "seq"), None)),
        check_vma=False,
    )
```

```python
import jax
import jax.numpy as jnp
from jax import lax
from jax.sharding import PartitionSpec as P

RATES = 16


highest = lax.Precision.HIGHEST


def partner(value, axis, apart):
    mask = 2**apart
    pairs = [(source, source ^ mask) for source in range(lax.axis_size(axis))]
    return lax.ppermute(value, axis, pairs)


def rate_logs():
    ranks = jnp.arange(RATES).astype(jnp.float32)
    return -0.0001 * jnp.power(jnp.float32(500.0), ranks / (RATES - 1))


def decay_parts(logrates, flags):
    length = flags.shape[0]
    sums = jnp.cumsum(logrates, axis=1)
    segment = jnp.cumsum(flags)
    order = jnp.arange(length)
    inside = (segment[:, None] == segment[None, :]) & (order[:, None] >= order[None, :])
    spread = sums[:, :, None] - sums[:, None, :]
    lower_mat = jnp.where(inside[None], jnp.exp(jnp.where(inside[None], spread, 0.0)), 0.0)
    cumulative = jnp.where((segment == 0)[None, :], jnp.exp(sums), 0.0)
    end_weight = lower_mat[:, length - 1, :]
    return (lower_mat, cumulative, end_weight)


def join_pairs(earlier, later):
    return (earlier[0] * later[0], later[0][:, None, None] * earlier[1] + later[1])


def pick_pair(flag, first, second):
    return (jnp.where(flag, first[0], second[0]), jnp.where(flag, first[1], second[1]))


def combine_levels(own, identity, from_higher, bits):
    position = lax.axis_index("seq")
    prefix = identity
    total = own
    for bit in bits:
        other = partner(total, "seq", bit)
        high_half = position // (1 << bit) % 2 == 1
        takes_other = jnp.logical_not(high_half) if from_higher else high_half
        prefix = pick_pair(takes_other, join_pairs(other, prefix), prefix)
        total = pick_pair(takes_other, join_pairs(other, total), join_pairs(total, other))
    return prefix, total


def identity_pair(heads, shape):
    return (jnp.ones((heads,), jnp.float32), jnp.zeros((heads,) + shape, jnp.float32))


def combine_chain(own, from_higher):
    heads = own[0].shape[0]
    half = heads // 2
    shape = own[1].shape[1:]
    core = lax.axis_index("seq") % 2
    levels = lax.axis_size("seq").bit_length() - 1
    in_chip, chip_total = combine_levels(own, identity_pair(heads, shape), from_higher, [0])
    start = core * half
    mine = tuple(lax.dynamic_slice_in_dim(part, start, half, 0) for part in chip_total)
    across, unused = combine_levels(mine, identity_pair(half, shape), from_higher, range(1, levels))
    sibling = partner(across, "seq", 0)
    first = pick_pair(core == 0, across, sibling)
    second = pick_pair(core == 0, sibling, across)
    full = tuple(jnp.concatenate([a, b], axis=0) for a, b in zip(first, second))
    return join_pairs(full, in_chip)


def scatter_sum(product):
    dp_size, seq_size = lax.axis_size("dp"), lax.axis_size("seq")
    seq_bits = seq_size.bit_length() - 1
    dp_bits = dp_size.bit_length() - 1
    bits = seq_bits + dp_bits
    rows, cols = product.shape
    block = rows // (dp_size * seq_size)
    seq_pos, dp_pos = lax.axis_index("seq"), lax.axis_index("dp")
    near = [0, 1, 3, seq_bits + 1, 2, 4, seq_bits + 2, seq_bits, seq_bits + 3]
    order = []
    for b in near + list(range(bits)):
        if b < bits and b not in order:
            order.append(b)
    buf = product.reshape((2,) * bits + (block * cols,))
    buf = buf.transpose([bits - 1 - b for b in order] + [bits]).reshape(2**bits, block * cols)
    for bit in order:
        count = buf.shape[0] // 2
        low, high = buf[:count], buf[count:]
        if bit < seq_bits:
            axis, apart, mine = "seq", bit, seq_pos // (1 << bit) % 2 == 1
        else:
            axis, apart, mine = "dp", bit - seq_bits, dp_pos // (1 << (bit - seq_bits)) % 2 == 1
        keep = jnp.where(mine, high, low)
        send = jnp.where(mine, low, high)
        buf = keep + partner(send, axis, apart)
    return buf.reshape(block, cols)


def local(normed, values, cotangent, w_bc, rate_index, starts):
    hidden = normed[0]
    length = hidden.shape[0]
    heads = rate_index.shape[1]
    width = values.shape[2]
    head_dim = width // heads
    state = w_bc.shape[1] // 2
    proj = jnp.dot(hidden, w_bc, preferred_element_type=jnp.float32).astype(jnp.bfloat16)
    bmat = proj[:, :state].astype(jnp.float32)
    cmat = proj[:, state:].astype(jnp.float32)
    levels_table = rate_logs()
    matches = rate_index[0][:, :, None] == jnp.arange(RATES)[None, None, :]
    logrates = jnp.sum(jnp.where(matches, levels_table[None, None, :], 0.0), axis=2)
    lower_mat, cumulative, end_weight = decay_parts(logrates, starts[0])
    vals = values[0].astype(jnp.float32).reshape(length, heads, head_dim)
    cots = cotangent[0].astype(jnp.float32).reshape(length, heads, head_dim)
    decay_total = cumulative[:, -1]
    ends = jnp.einsum("hk,kn,khp->hnp", end_weight, bmat, vals, precision=highest)
    feeds = jnp.einsum("hk,kn,khp->hnp", cumulative, cmat, cots, precision=highest)
    before = combine_chain((decay_total, ends), False)[1]
    after = combine_chain((decay_total, feeds), True)[1]
    scores = jnp.dot(cmat, bmat.T, precision=highest)
    mixed = lower_mat * scores[None]
    grad_vals = jnp.einsum("hts,thp->shp", mixed, cots, precision=highest)
    grad_vals = grad_vals + end_weight.T[:, :, None] * jnp.einsum(
        "sn,hnp->shp", bmat, after, precision=highest
    )
    paired = lower_mat * jnp.einsum("thp,shp->hts", cots, vals, precision=highest)
    grad_b = jnp.einsum("hts,tn->sn", paired, cmat, precision=highest)
    grad_b = grad_b + jnp.einsum("hs,shp,hnp->sn", end_weight, vals, after, precision=highest)
    grad_c = jnp.einsum("hts,sn->tn", paired, bmat, precision=highest)
    grad_c = grad_c + jnp.einsum("ht,thp,hnp->tn", cumulative, cots, before, precision=highest)
    grad_values = grad_vals.reshape(length, width).astype(jnp.bfloat16)[None]
    grad_bc = jnp.concatenate([grad_b, grad_c], axis=1).astype(jnp.bfloat16)
    scale = 1.0 / (lax.axis_size("dp") * lax.axis_size("seq") * length)
    product = lax.dot_general(
        hidden, grad_bc, (((0,), (0,)), ((), ())), preferred_element_type=jnp.float32
    )
    grad_wbc = scatter_sum(product) * scale
    return (grad_values, grad_wbc)


def solution(mesh):
    placed = (
        P("dp", "seq", None),
        P("dp", "seq", None),
        P("dp", "seq", None),
        P(),
        P("dp", None, "seq"),
        P("dp", "seq"),
    )
    return jax.shard_map(
        local,
        mesh=mesh,
        in_specs=placed,
        out_specs=(P("dp", "seq", None), P(("dp", "seq"), None)),
        check_vma=False,
    )
```

```python
import functools

import jax
import jax.numpy as jnp
from jax import lax
from jax.experimental import pallas as pl
from jax.experimental.pallas import tpu as pltpu
from jax.sharding import PartitionSpec as P

MESH = pl.DeviceIdType.MESH

RATES = 16


highest = lax.Precision.HIGHEST


def partner(value, axis, apart):
    mask = 2**apart
    pairs = [(source, source ^ mask) for source in range(lax.axis_size(axis))]
    return lax.ppermute(value, axis, pairs)


def rate_logs():
    ranks = jnp.arange(RATES).astype(jnp.float32)
    return -0.0001 * jnp.power(jnp.float32(500.0), ranks / (RATES - 1))


def decay_parts(logrates, flags):
    length = flags.shape[0]
    sums = jnp.cumsum(logrates, axis=1)
    segment = jnp.cumsum(flags)
    order = jnp.arange(length)
    inside = (segment[:, None] == segment[None, :]) & (order[:, None] >= order[None, :])
    spread = sums[:, :, None] - sums[:, None, :]
    lower_mat = jnp.where(inside[None], jnp.exp(jnp.where(inside[None], spread, 0.0)), 0.0)
    cumulative = jnp.where((segment == 0)[None, :], jnp.exp(sums), 0.0)
    end_weight = lower_mat[:, length - 1, :]
    return (lower_mat, cumulative, end_weight)


def join_pairs(earlier, later):
    return (earlier[0] * later[0], later[0][:, None, None] * earlier[1] + later[1])


def pick_pair(flag, first, second):
    return (jnp.where(flag, first[0], second[0]), jnp.where(flag, first[1], second[1]))


def combine_levels(own, identity, from_higher, bits):
    position = lax.axis_index("seq")
    prefix = identity
    total = own
    for bit in bits:
        other = partner(total, "seq", bit)
        high_half = position // (1 << bit) % 2 == 1
        takes_other = jnp.logical_not(high_half) if from_higher else high_half
        prefix = pick_pair(takes_other, join_pairs(other, prefix), prefix)
        total = pick_pair(takes_other, join_pairs(other, total), join_pairs(total, other))
    return prefix, total


def identity_pair(heads, shape):
    return (jnp.ones((heads,), jnp.float32), jnp.zeros((heads,) + shape, jnp.float32))


def combine_chain(own, from_higher):
    heads = own[0].shape[0]
    half = heads // 2
    shape = own[1].shape[1:]
    core = lax.axis_index("seq") % 2
    levels = lax.axis_size("seq").bit_length() - 1
    in_chip, chip_total = combine_levels(own, identity_pair(heads, shape), from_higher, [0])
    start = core * half
    mine = tuple(lax.dynamic_slice_in_dim(part, start, half, 0) for part in chip_total)
    across, unused = combine_levels(mine, identity_pair(half, shape), from_higher, range(1, levels))
    sibling = partner(across, "seq", 0)
    first = pick_pair(core == 0, across, sibling)
    second = pick_pair(core == 0, sibling, across)
    full = tuple(jnp.concatenate([a, b], axis=0) for a, b in zip(first, second))
    return join_pairs(full, in_chip)


def flat_bit_order(seq_bits, bits):
    near = [0, 1, 3, seq_bits + 1, 2, 4, seq_bits + 2, seq_bits, seq_bits + 3]
    order = []
    for b in near + list(range(bits)):
        if b < bits and b not in order:
            order.append(b)
    return order


def halving_kernel(seq_bits, order, buf_ref, out_ref, *scratch):
    steps = len(order)
    recvs = scratch[:steps]
    accs = scratch[steps:2 * steps - 1] + (out_ref,)
    send_sem, recv_sem = scratch[2 * steps - 1], scratch[2 * steps]
    stages = scratch[2 * steps + 1:]
    seq_pos, dp_pos = lax.axis_index("seq"), lax.axis_index("dp")
    targets = []
    for bit in order:
        if bit < seq_bits:
            mask = 1 << bit
            mine = seq_pos // mask % 2
            targets.append((mine, (dp_pos, seq_pos + mask - 2 * mask * mine)))
        else:
            mask = 1 << (bit - seq_bits)
            mine = dp_pos // mask % 2
            targets.append((mine, (dp_pos + mask - 2 * mask * mine, seq_pos)))
    barrier = pltpu.get_barrier_semaphore()
    for unused, device in targets:
        pl.semaphore_signal(barrier, inc=1, device_id=device, device_id_type=MESH)
    pl.semaphore_wait(barrier, steps)
    current = buf_ref
    staged = 0
    for step in range(steps):
        mine, device = targets[step]
        half = recvs[step].shape[0]
        if half % 8 == 0:
            source = current.at[pl.ds(pl.multiple_of((1 - mine) * half, 8), half)]
        else:
            source = stages[staged]
            staged += 1
            source[...] = jnp.where(mine == 1, current[0:half], current[half:2 * half])
        copy = pltpu.make_async_remote_copy(
            src_ref=source,
            dst_ref=recvs[step],
            send_sem=send_sem.at[step],
            recv_sem=recv_sem.at[step],
            device_id=device,
            device_id_type=MESH,
        )
        copy.start()
        if half % 8 == 0:
            keep = current[pl.ds(pl.multiple_of(mine * half, 8), half)]
        else:
            keep = jnp.where(mine == 1, current[half:2 * half], current[0:half])
        copy.wait()
        accs[step][...] = keep + recvs[step][...]
        current = accs[step]


def scatter_sum(product):
    dp_size, seq_size = lax.axis_size("dp"), lax.axis_size("seq")
    seq_bits = seq_size.bit_length() - 1
    bits = seq_bits + dp_size.bit_length() - 1
    rows, cols = product.shape
    block = rows // (dp_size * seq_size)
    order = flat_bit_order(seq_bits, bits)
    buf = product.reshape((2,) * bits + (block * cols,))
    buf = buf.transpose([bits - 1 - b for b in order] + [bits]).reshape(2**bits, block * cols)
    sizes = [2 ** (bits - 1 - step) for step in range(bits)]
    scratch = [pltpu.VMEM((size, block * cols), jnp.float32) for size in sizes]
    scratch += [pltpu.VMEM((size, block * cols), jnp.float32) for size in sizes[:-1]]
    scratch += [pltpu.SemaphoreType.DMA((bits,)), pltpu.SemaphoreType.DMA((bits,))]
    scratch += [pltpu.VMEM((size, block * cols), jnp.float32) for size in sizes if size % 8]
    out = pl.pallas_call(
        functools.partial(halving_kernel, seq_bits, order),
        out_shape=jax.ShapeDtypeStruct((1, block * cols), jnp.float32),
        in_specs=[pl.BlockSpec(memory_space=pltpu.VMEM)],
        out_specs=pl.BlockSpec(memory_space=pltpu.VMEM),
        scratch_shapes=scratch,
        compiler_params=pltpu.CompilerParams(collective_id=0, has_side_effects=True),
    )(buf)
    return out.reshape(block, cols)


def local(normed, values, cotangent, w_bc, rate_index, starts):
    hidden = normed[0]
    length = hidden.shape[0]
    heads = rate_index.shape[1]
    width = values.shape[2]
    head_dim = width // heads
    state = w_bc.shape[1] // 2
    proj = jnp.dot(hidden, w_bc, preferred_element_type=jnp.float32).astype(jnp.bfloat16)
    bmat = proj[:, :state].astype(jnp.float32)
    cmat = proj[:, state:].astype(jnp.float32)
    levels_table = rate_logs()
    matches = rate_index[0][:, :, None] == jnp.arange(RATES)[None, None, :]
    logrates = jnp.sum(jnp.where(matches, levels_table[None, None, :], 0.0), axis=2)
    lower_mat, cumulative, end_weight = decay_parts(logrates, starts[0])
    vals = values[0].astype(jnp.float32).reshape(length, heads, head_dim)
    cots = cotangent[0].astype(jnp.float32).reshape(length, heads, head_dim)
    decay_total = cumulative[:, -1]
    ends = jnp.einsum("hk,kn,khp->hnp", end_weight, bmat, vals, precision=highest)
    feeds = jnp.einsum("hk,kn,khp->hnp", cumulative, cmat, cots, precision=highest)
    before = combine_chain((decay_total, ends), False)[1]
    after = combine_chain((decay_total, feeds), True)[1]
    scores = jnp.dot(cmat, bmat.T, precision=highest)
    mixed = lower_mat * scores[None]
    grad_vals = jnp.einsum("hts,thp->shp", mixed, cots, precision=highest)
    grad_vals = grad_vals + end_weight.T[:, :, None] * jnp.einsum(
        "sn,hnp->shp", bmat, after, precision=highest
    )
    paired = lower_mat * jnp.einsum("thp,shp->hts", cots, vals, precision=highest)
    grad_b = jnp.einsum("hts,tn->sn", paired, cmat, precision=highest)
    grad_b = grad_b + jnp.einsum("hs,shp,hnp->sn", end_weight, vals, after, precision=highest)
    grad_c = jnp.einsum("hts,sn->tn", paired, bmat, precision=highest)
    grad_c = grad_c + jnp.einsum("ht,thp,hnp->tn", cumulative, cots, before, precision=highest)
    grad_values = grad_vals.reshape(length, width).astype(jnp.bfloat16)[None]
    grad_bc = jnp.concatenate([grad_b, grad_c], axis=1).astype(jnp.bfloat16)
    scale = 1.0 / (lax.axis_size("dp") * lax.axis_size("seq") * length)
    product = lax.dot_general(
        hidden, grad_bc, (((0,), (0,)), ((), ())), preferred_element_type=jnp.float32
    )
    grad_wbc = scatter_sum(product) * scale
    return (grad_values, grad_wbc)


def solution(mesh):
    placed = (
        P("dp", "seq", None),
        P("dp", "seq", None),
        P("dp", "seq", None),
        P(),
        P("dp", None, "seq"),
        P("dp", "seq"),
    )
    return jax.shard_map(
        local,
        mesh=mesh,
        in_specs=placed,
        out_specs=(P("dp", "seq", None), P(("dp", "seq"), None)),
        check_vma=False,
    )
```

```python
import functools

import jax
import jax.numpy as jnp
from jax import lax
from jax.experimental import pallas as pl
from jax.experimental.pallas import tpu as pltpu
from jax.sharding import PartitionSpec as P

MESH = pl.DeviceIdType.MESH

RATES = 16


highest = lax.Precision.HIGHEST


def partner(value, axis, apart):
    mask = 2**apart
    pairs = [(source, source ^ mask) for source in range(lax.axis_size(axis))]
    return lax.ppermute(value, axis, pairs)


def rate_logs():
    ranks = jnp.arange(RATES).astype(jnp.float32)
    return -0.0001 * jnp.power(jnp.float32(500.0), ranks / (RATES - 1))


def decay_parts(logrates, flags):
    length = flags.shape[0]
    sums = jnp.cumsum(logrates, axis=1)
    segment = jnp.cumsum(flags)
    order = jnp.arange(length)
    inside = (segment[:, None] == segment[None, :]) & (order[:, None] >= order[None, :])
    spread = sums[:, :, None] - sums[:, None, :]
    lower_mat = jnp.where(inside[None], jnp.exp(jnp.where(inside[None], spread, 0.0)), 0.0)
    cumulative = jnp.where((segment == 0)[None, :], jnp.exp(sums), 0.0)
    end_weight = lower_mat[:, length - 1, :]
    return (lower_mat, cumulative, end_weight)


def join_pairs(earlier, later):
    return (earlier[0] * later[0], later[0][:, None, None] * earlier[1] + later[1])


def pick_pair(flag, first, second):
    return (jnp.where(flag, first[0], second[0]), jnp.where(flag, first[1], second[1]))


def combine_levels(state, from_higher, bits):
    position = lax.axis_index("seq")
    prefix, total = state
    for bit in bits:
        other = partner(total, "seq", bit)
        high_half = position // (1 << bit) % 2 == 1
        takes_other = jnp.logical_not(high_half) if from_higher else high_half
        prefix = pick_pair(takes_other, join_pairs(other, prefix), prefix)
        total = pick_pair(takes_other, join_pairs(other, total), join_pairs(total, other))
    return prefix, total


def identity_pair(heads, shape):
    return (jnp.ones((heads,), jnp.float32), jnp.zeros((heads,) + shape, jnp.float32))


def heads_of(pair, begin, end):
    return (pair[0][begin:end], pair[1][begin:end])


def combine_chains(owns):
    heads = owns[0][0].shape[0]
    half = heads // 2
    quarter = half // 2
    shape = owns[0][1].shape[1:]
    core = lax.axis_index("seq") % 2
    levels = lax.axis_size("seq").bit_length() - 1
    middle = 1 + (levels - 1) // 2
    directions = (False, True)
    in_chips, mines = [], []
    for own, from_higher in zip(owns, directions):
        in_chip, chip_total = combine_levels((identity_pair(heads, shape), own), from_higher, [0])
        in_chips.append(in_chip)
        mines.append(tuple(lax.dynamic_slice_in_dim(part, core * half, half, 0) for part in chip_total))
    firsts = [
        combine_levels((identity_pair(quarter, shape), heads_of(mine, 0, quarter)), from_higher, range(1, middle))
        for mine, from_higher in zip(mines, directions)
    ]
    seconds = [heads_of(mine, quarter, half) for mine in mines]
    seconds, unused = lax.optimization_barrier((seconds, [first[1] for first in firsts]))
    seconds = [
        combine_levels((identity_pair(half - quarter, shape), second), from_higher, range(1, middle))
        for second, from_higher in zip(seconds, directions)
    ]
    firsts = [combine_levels(first, fh, range(middle, levels)) for first, fh in zip(firsts, directions)]
    seconds = [combine_levels(second, fh, range(middle, levels)) for second, fh in zip(seconds, directions)]
    results = []
    for first, second, in_chip in zip(firsts, seconds, in_chips):
        across = tuple(jnp.concatenate([a, b], axis=0) for a, b in zip(first[0], second[0]))
        sibling = partner(across, "seq", 0)
        low = pick_pair(core == 0, across, sibling)
        high = pick_pair(core == 0, sibling, across)
        full = tuple(jnp.concatenate([a, b], axis=0) for a, b in zip(low, high))
        results.append(join_pairs(full, in_chip))
    return results


def flat_bit_order(seq_bits, bits):
    near = [0, 1, 3, seq_bits + 1, 2, 4, seq_bits + 2, seq_bits, seq_bits + 3]
    order = []
    for b in near + list(range(bits)):
        if b < bits and b not in order:
            order.append(b)
    return order


def halving_kernel(seq_bits, order, buf_ref, out_ref, *scratch):
    steps = len(order)
    recvs = scratch[:steps]
    accs = scratch[steps:2 * steps - 1] + (out_ref,)
    send_sem, recv_sem = scratch[2 * steps - 1], scratch[2 * steps]
    stages = scratch[2 * steps + 1:]
    seq_pos, dp_pos = lax.axis_index("seq"), lax.axis_index("dp")
    targets = []
    for bit in order:
        if bit < seq_bits:
            mask = 1 << bit
            mine = seq_pos // mask % 2
            targets.append((mine, (dp_pos, seq_pos + mask - 2 * mask * mine)))
        else:
            mask = 1 << (bit - seq_bits)
            mine = dp_pos // mask % 2
            targets.append((mine, (dp_pos + mask - 2 * mask * mine, seq_pos)))
    barrier = pltpu.get_barrier_semaphore()
    for unused, device in targets:
        pl.semaphore_signal(barrier, inc=1, device_id=device, device_id_type=MESH)
    pl.semaphore_wait(barrier, steps)
    current = buf_ref
    staged = 0
    for step in range(steps):
        mine, device = targets[step]
        half = recvs[step].shape[0]
        if half % 8 == 0:
            source = current.at[pl.ds(pl.multiple_of((1 - mine) * half, 8), half)]
        else:
            source = stages[staged]
            staged += 1
            source[...] = jnp.where(mine == 1, current[0:half], current[half:2 * half])
        copy = pltpu.make_async_remote_copy(
            src_ref=source,
            dst_ref=recvs[step],
            send_sem=send_sem.at[step],
            recv_sem=recv_sem.at[step],
            device_id=device,
            device_id_type=MESH,
        )
        copy.start()
        if half % 8 == 0:
            keep = current[pl.ds(pl.multiple_of(mine * half, 8), half)]
        else:
            keep = jnp.where(mine == 1, current[half:2 * half], current[0:half])
        copy.wait()
        accs[step][...] = keep + recvs[step][...]
        current = accs[step]


def scatter_sum(product):
    dp_size, seq_size = lax.axis_size("dp"), lax.axis_size("seq")
    seq_bits = seq_size.bit_length() - 1
    bits = seq_bits + dp_size.bit_length() - 1
    rows, cols = product.shape
    block = rows // (dp_size * seq_size)
    order = flat_bit_order(seq_bits, bits)
    buf = product.reshape((2,) * bits + (block * cols,))
    buf = buf.transpose([bits - 1 - b for b in order] + [bits]).reshape(2**bits, block * cols)
    sizes = [2 ** (bits - 1 - step) for step in range(bits)]
    scratch = [pltpu.VMEM((size, block * cols), jnp.float32) for size in sizes]
    scratch += [pltpu.VMEM((size, block * cols), jnp.float32) for size in sizes[:-1]]
    scratch += [pltpu.SemaphoreType.DMA((bits,)), pltpu.SemaphoreType.DMA((bits,))]
    scratch += [pltpu.VMEM((size, block * cols), jnp.float32) for size in sizes if size % 8]
    out = pl.pallas_call(
        functools.partial(halving_kernel, seq_bits, order),
        out_shape=jax.ShapeDtypeStruct((1, block * cols), jnp.float32),
        in_specs=[pl.BlockSpec(memory_space=pltpu.VMEM)],
        out_specs=pl.BlockSpec(memory_space=pltpu.VMEM),
        scratch_shapes=scratch,
        compiler_params=pltpu.CompilerParams(collective_id=0, has_side_effects=True),
    )(buf)
    return out.reshape(block, cols)


def local(normed, values, cotangent, w_bc, rate_index, starts):
    hidden = normed[0]
    length = hidden.shape[0]
    heads = rate_index.shape[1]
    width = values.shape[2]
    head_dim = width // heads
    state = w_bc.shape[1] // 2
    proj = jnp.dot(hidden, w_bc, preferred_element_type=jnp.float32).astype(jnp.bfloat16)
    bmat = proj[:, :state].astype(jnp.float32)
    cmat = proj[:, state:].astype(jnp.float32)
    levels_table = rate_logs()
    matches = rate_index[0][:, :, None] == jnp.arange(RATES)[None, None, :]
    logrates = jnp.sum(jnp.where(matches, levels_table[None, None, :], 0.0), axis=2)
    lower_mat, cumulative, end_weight = decay_parts(logrates, starts[0])
    vals = values[0].astype(jnp.float32).reshape(length, heads, head_dim)
    cots = cotangent[0].astype(jnp.float32).reshape(length, heads, head_dim)
    decay_total = cumulative[:, -1]
    ends = jnp.einsum("hk,kn,khp->hnp", end_weight, bmat, vals, precision=highest)
    feeds = jnp.einsum("hk,kn,khp->hnp", cumulative, cmat, cots, precision=highest)
    before_pair, after_pair = combine_chains([(decay_total, ends), (decay_total, feeds)])
    before, after = before_pair[1], after_pair[1]
    scores = jnp.dot(cmat, bmat.T, precision=highest)
    mixed = lower_mat * scores[None]
    grad_vals = jnp.einsum("hts,thp->shp", mixed, cots, precision=highest)
    grad_vals = grad_vals + end_weight.T[:, :, None] * jnp.einsum(
        "sn,hnp->shp", bmat, after, precision=highest
    )
    paired = lower_mat * jnp.einsum("thp,shp->hts", cots, vals, precision=highest)
    grad_b = jnp.einsum("hts,tn->sn", paired, cmat, precision=highest)
    grad_b = grad_b + jnp.einsum("hs,shp,hnp->sn", end_weight, vals, after, precision=highest)
    grad_c = jnp.einsum("hts,sn->tn", paired, bmat, precision=highest)
    grad_c = grad_c + jnp.einsum("ht,thp,hnp->tn", cumulative, cots, before, precision=highest)
    grad_values = grad_vals.reshape(length, width).astype(jnp.bfloat16)[None]
    grad_bc = jnp.concatenate([grad_b, grad_c], axis=1).astype(jnp.bfloat16)
    scale = 1.0 / (lax.axis_size("dp") * lax.axis_size("seq") * length)
    product = lax.dot_general(
        hidden, grad_bc, (((0,), (0,)), ((), ())), preferred_element_type=jnp.float32
    )
    grad_wbc = scatter_sum(product) * scale
    return (grad_values, grad_wbc)


def solution(mesh):
    placed = (
        P("dp", "seq", None),
        P("dp", "seq", None),
        P("dp", "seq", None),
        P(),
        P("dp", None, "seq"),
        P("dp", "seq"),
    )
    return jax.shard_map(
        local,
        mesh=mesh,
        in_specs=placed,
        out_specs=(P("dp", "seq", None), P(("dp", "seq"), None)),
        check_vma=False,
    )
```

```python
import functools

import jax
import jax.numpy as jnp
from jax import lax
from jax.experimental import pallas as pl
from jax.experimental.pallas import tpu as pltpu
from jax.sharding import PartitionSpec as P

MESH = pl.DeviceIdType.MESH

RATES = 16


highest = lax.Precision.HIGHEST


def partner(value, axis, apart):
    mask = 2**apart
    pairs = [(source, source ^ mask) for source in range(lax.axis_size(axis))]
    return lax.ppermute(value, axis, pairs)


def rate_logs():
    ranks = jnp.arange(RATES).astype(jnp.float32)
    return -0.0001 * jnp.power(jnp.float32(500.0), ranks / (RATES - 1))


def decay_parts(logrates, flags):
    length = flags.shape[0]
    sums = jnp.cumsum(logrates, axis=1)
    segment = jnp.cumsum(flags)
    order = jnp.arange(length)
    inside = (segment[:, None] == segment[None, :]) & (order[:, None] >= order[None, :])
    spread = sums[:, :, None] - sums[:, None, :]
    lower_mat = jnp.where(inside[None], jnp.exp(jnp.where(inside[None], spread, 0.0)), 0.0)
    cumulative = jnp.where((segment == 0)[None, :], jnp.exp(sums), 0.0)
    end_weight = lower_mat[:, length - 1, :]
    return (lower_mat, cumulative, end_weight)


def join_pairs(earlier, later):
    return (earlier[0] * later[0], later[0][:, None, None] * earlier[1] + later[1])


def pick_pair(flag, first, second):
    return (jnp.where(flag, first[0], second[0]), jnp.where(flag, first[1], second[1]))


def combine_levels(state, from_higher, bits):
    position = lax.axis_index("seq")
    prefix, total = state
    for bit in bits:
        other = partner(total, "seq", bit)
        high_half = position // (1 << bit) % 2 == 1
        takes_other = jnp.logical_not(high_half) if from_higher else high_half
        prefix = pick_pair(takes_other, join_pairs(other, prefix), prefix)
        total = pick_pair(takes_other, join_pairs(other, total), join_pairs(total, other))
    return prefix, total


def identity_pair(heads, shape):
    return (jnp.ones((heads,), jnp.float32), jnp.zeros((heads,) + shape, jnp.float32))


def chain_kernel(bits, shift, a_ref, e_ref, pa_ref, pe_ref, tot_a, tot_e, recv_a, recv_e, send_sem, recv_sem):
    seq_pos, dp_pos = lax.axis_index("seq"), lax.axis_index("dp")
    levels = len(bits)
    chains, groups = e_ref.shape[0], e_ref.shape[1]
    highs, partners = [], []
    for bit in bits:
        mask = 1 << bit
        up = seq_pos // mask % 2
        highs.append(up == 1)
        partners.append((dp_pos, seq_pos + mask - 2 * mask * up))
    barrier = pltpu.get_barrier_semaphore()
    for device in partners:
        pl.semaphore_signal(barrier, inc=1, device_id=device, device_id_type=MESH)
    pl.semaphore_wait(barrier, levels)
    pa_ref[...] = jnp.ones(pa_ref.shape, jnp.float32)
    pe_ref[...] = jnp.zeros(pe_ref.shape, jnp.float32)
    for slot in range(levels + shift * (groups - 1)):
        active = [(g, slot - shift * g) for g in range(groups) if 0 <= slot - shift * g < levels]
        work = []
        for g, lev in active:
            src_a = a_ref.at[g] if lev == 0 else tot_a.at[(lev - 1) % 2, g]
            src_e = [e_ref.at[c, g] if lev == 0 else tot_e.at[(lev - 1) % 2, c, g] for c in range(chains)]
            pairs = [(src_a, recv_a.at[lev, g])] + [(src_e[c], recv_e.at[lev, c, g]) for c in range(chains)]
            copies = []
            for k, (source, target) in enumerate(pairs):
                index = (lev * groups + g) * (chains + 1) + k
                copy = pltpu.make_async_remote_copy(
                    src_ref=source,
                    dst_ref=target,
                    send_sem=send_sem.at[index],
                    recv_sem=recv_sem.at[index],
                    device_id=partners[lev],
                    device_id_type=MESH,
                )
                copy.start()
                copies.append(copy)
            work.append((g, lev, src_a, src_e, copies))
        for g, lev, src_a, src_e, copies in work:
            for copy in copies:
                copy.wait()
            o_a = recv_a[lev, g]
            t_a = src_a[...]
            last = lev == levels - 1
            if not last:
                tot_a[lev % 2, g] = o_a * t_a
            for c in range(chains):
                takes = jnp.logical_not(highs[lev]) if c == 1 else highs[lev]
                o_e = recv_e[lev, c, g]
                p_a = pa_ref[c, g]
                p_e = pe_ref[c, g]
                pe_ref[c, g] = jnp.where(takes, p_a * o_e + p_e, p_e)
                pa_ref[c, g] = jnp.where(takes, o_a * p_a, p_a)
                if not last:
                    t_e = src_e[c][...]
                    tot_e[lev % 2, c, g] = jnp.where(takes, t_a * o_e + t_e, o_a * t_e + o_e)


def chip_scan(mines):
    heads = mines[0][0].shape[0]
    groups = 2
    quarter = heads // groups
    state, width = mines[0][1].shape[1:]
    rows = state * width // 128
    levels = lax.axis_size("seq").bit_length() - 1
    bits = tuple(range(1, levels))
    shift = (levels - 1) // 2
    a_in = jnp.broadcast_to(mines[0][0].reshape(groups, quarter, 1, 1), (groups, quarter, 1, 128))
    e_in = jnp.stack([mine[1].reshape(groups, quarter, rows, 128) for mine in mines])
    chains = len(mines)
    copies = len(bits) * groups * (chains + 1)
    pa, pe = pl.pallas_call(
        functools.partial(chain_kernel, bits, shift),
        out_shape=(
            jax.ShapeDtypeStruct((chains, groups, quarter, 1, 128), jnp.float32),
            jax.ShapeDtypeStruct((chains, groups, quarter, rows, 128), jnp.float32),
        ),
        in_specs=[pl.BlockSpec(memory_space=pltpu.VMEM)] * 2,
        out_specs=(pl.BlockSpec(memory_space=pltpu.VMEM), pl.BlockSpec(memory_space=pltpu.VMEM)),
        scratch_shapes=[
            pltpu.VMEM((2, groups, quarter, 1, 128), jnp.float32),
            pltpu.VMEM((2, chains, groups, quarter, rows, 128), jnp.float32),
            pltpu.VMEM((len(bits), groups, quarter, 1, 128), jnp.float32),
            pltpu.VMEM((len(bits), chains, groups, quarter, rows, 128), jnp.float32),
            pltpu.SemaphoreType.DMA((copies,)),
            pltpu.SemaphoreType.DMA((copies,)),
        ],
        compiler_params=pltpu.CompilerParams(collective_id=1, has_side_effects=True),
    )(a_in, e_in)
    return [(pa[c, :, :, 0, 0].reshape(heads), pe[c].reshape(heads, state, width)) for c in range(chains)]


def combine_chains(owns):
    heads = owns[0][0].shape[0]
    half = heads // 2
    shape = owns[0][1].shape[1:]
    core = lax.axis_index("seq") % 2
    directions = (False, True)
    in_chips, mines = [], []
    for own, from_higher in zip(owns, directions):
        in_chip, chip_total = combine_levels((identity_pair(heads, shape), own), from_higher, [0])
        in_chips.append(in_chip)
        mines.append(tuple(lax.dynamic_slice_in_dim(part, core * half, half, 0) for part in chip_total))
    results = []
    for across, in_chip in zip(chip_scan(mines), in_chips):
        sibling = partner(across, "seq", 0)
        low = pick_pair(core == 0, across, sibling)
        high = pick_pair(core == 0, sibling, across)
        full = tuple(jnp.concatenate([a, b], axis=0) for a, b in zip(low, high))
        results.append(join_pairs(full, in_chip))
    return results


def flat_bit_order(seq_bits, bits):
    near = [0, 1, 3, seq_bits + 1, 2, 4, seq_bits + 2, seq_bits, seq_bits + 3]
    order = []
    for b in near + list(range(bits)):
        if b < bits and b not in order:
            order.append(b)
    return order


def halving_kernel(seq_bits, order, buf_ref, out_ref, *scratch):
    steps = len(order)
    recvs = scratch[:steps]
    accs = scratch[steps:2 * steps - 1] + (out_ref,)
    send_sem, recv_sem = scratch[2 * steps - 1], scratch[2 * steps]
    stages = scratch[2 * steps + 1:]
    seq_pos, dp_pos = lax.axis_index("seq"), lax.axis_index("dp")
    targets = []
    for bit in order:
        if bit < seq_bits:
            mask = 1 << bit
            mine = seq_pos // mask % 2
            targets.append((mine, (dp_pos, seq_pos + mask - 2 * mask * mine)))
        else:
            mask = 1 << (bit - seq_bits)
            mine = dp_pos // mask % 2
            targets.append((mine, (dp_pos + mask - 2 * mask * mine, seq_pos)))
    barrier = pltpu.get_barrier_semaphore()
    for unused, device in targets:
        pl.semaphore_signal(barrier, inc=1, device_id=device, device_id_type=MESH)
    pl.semaphore_wait(barrier, steps)
    current = buf_ref
    staged = 0
    for step in range(steps):
        mine, device = targets[step]
        half = recvs[step].shape[0]
        if half % 8 == 0:
            source = current.at[pl.ds(pl.multiple_of((1 - mine) * half, 8), half)]
        else:
            source = stages[staged]
            staged += 1
            source[...] = jnp.where(mine == 1, current[0:half], current[half:2 * half])
        copy = pltpu.make_async_remote_copy(
            src_ref=source,
            dst_ref=recvs[step],
            send_sem=send_sem.at[step],
            recv_sem=recv_sem.at[step],
            device_id=device,
            device_id_type=MESH,
        )
        copy.start()
        if half % 8 == 0:
            keep = current[pl.ds(pl.multiple_of(mine * half, 8), half)]
        else:
            keep = jnp.where(mine == 1, current[half:2 * half], current[0:half])
        copy.wait()
        accs[step][...] = keep + recvs[step][...]
        current = accs[step]


def scatter_sum(product):
    dp_size, seq_size = lax.axis_size("dp"), lax.axis_size("seq")
    seq_bits = seq_size.bit_length() - 1
    bits = seq_bits + dp_size.bit_length() - 1
    rows, cols = product.shape
    block = rows // (dp_size * seq_size)
    order = flat_bit_order(seq_bits, bits)
    buf = product.reshape((2,) * bits + (block * cols,))
    buf = buf.transpose([bits - 1 - b for b in order] + [bits]).reshape(2**bits, block * cols)
    sizes = [2 ** (bits - 1 - step) for step in range(bits)]
    scratch = [pltpu.VMEM((size, block * cols), jnp.float32) for size in sizes]
    scratch += [pltpu.VMEM((size, block * cols), jnp.float32) for size in sizes[:-1]]
    scratch += [pltpu.SemaphoreType.DMA((bits,)), pltpu.SemaphoreType.DMA((bits,))]
    scratch += [pltpu.VMEM((size, block * cols), jnp.float32) for size in sizes if size % 8]
    out = pl.pallas_call(
        functools.partial(halving_kernel, seq_bits, order),
        out_shape=jax.ShapeDtypeStruct((1, block * cols), jnp.float32),
        in_specs=[pl.BlockSpec(memory_space=pltpu.VMEM)],
        out_specs=pl.BlockSpec(memory_space=pltpu.VMEM),
        scratch_shapes=scratch,
        compiler_params=pltpu.CompilerParams(collective_id=0, has_side_effects=True),
    )(buf)
    return out.reshape(block, cols)


def local(normed, values, cotangent, w_bc, rate_index, starts):
    hidden = normed[0]
    length = hidden.shape[0]
    heads = rate_index.shape[1]
    width = values.shape[2]
    head_dim = width // heads
    state = w_bc.shape[1] // 2
    proj = jnp.dot(hidden, w_bc, preferred_element_type=jnp.float32).astype(jnp.bfloat16)
    bmat = proj[:, :state].astype(jnp.float32)
    cmat = proj[:, state:].astype(jnp.float32)
    levels_table = rate_logs()
    matches = rate_index[0][:, :, None] == jnp.arange(RATES)[None, None, :]
    logrates = jnp.sum(jnp.where(matches, levels_table[None, None, :], 0.0), axis=2)
    lower_mat, cumulative, end_weight = decay_parts(logrates, starts[0])
    vals = values[0].astype(jnp.float32).reshape(length, heads, head_dim)
    cots = cotangent[0].astype(jnp.float32).reshape(length, heads, head_dim)
    decay_total = cumulative[:, -1]
    ends = jnp.einsum("hk,kn,khp->hnp", end_weight, bmat, vals, precision=highest)
    feeds = jnp.einsum("hk,kn,khp->hnp", cumulative, cmat, cots, precision=highest)
    before_pair, after_pair = combine_chains([(decay_total, ends), (decay_total, feeds)])
    before, after = before_pair[1], after_pair[1]
    scores = jnp.dot(cmat, bmat.T, precision=highest)
    mixed = lower_mat * scores[None]
    grad_vals = jnp.einsum("hts,thp->shp", mixed, cots, precision=highest)
    grad_vals = grad_vals + end_weight.T[:, :, None] * jnp.einsum(
        "sn,hnp->shp", bmat, after, precision=highest
    )
    paired = lower_mat * jnp.einsum("thp,shp->hts", cots, vals, precision=highest)
    grad_b = jnp.einsum("hts,tn->sn", paired, cmat, precision=highest)
    grad_b = grad_b + jnp.einsum("hs,shp,hnp->sn", end_weight, vals, after, precision=highest)
    grad_c = jnp.einsum("hts,sn->tn", paired, bmat, precision=highest)
    grad_c = grad_c + jnp.einsum("ht,thp,hnp->tn", cumulative, cots, before, precision=highest)
    grad_values = grad_vals.reshape(length, width).astype(jnp.bfloat16)[None]
    grad_bc = jnp.concatenate([grad_b, grad_c], axis=1).astype(jnp.bfloat16)
    scale = 1.0 / (lax.axis_size("dp") * lax.axis_size("seq") * length)
    product = lax.dot_general(
        hidden, grad_bc, (((0,), (0,)), ((), ())), preferred_element_type=jnp.float32
    )
    grad_wbc = scatter_sum(product) * scale
    return (grad_values, grad_wbc)


def solution(mesh):
    placed = (
        P("dp", "seq", None),
        P("dp", "seq", None),
        P("dp", "seq", None),
        P(),
        P("dp", None, "seq"),
        P("dp", "seq"),
    )
    return jax.shard_map(
        local,
        mesh=mesh,
        in_specs=placed,
        out_specs=(P("dp", "seq", None), P(("dp", "seq"), None)),
        check_vma=False,
    )
```

```python
import functools

import jax
import jax.numpy as jnp
from jax import lax
from jax.experimental import pallas as pl
from jax.experimental.pallas import tpu as pltpu
from jax.sharding import PartitionSpec as P

MESH = pl.DeviceIdType.MESH

RATES = 16


highest = lax.Precision.HIGHEST


def partner(value, axis, apart):
    mask = 2**apart
    pairs = [(source, source ^ mask) for source in range(lax.axis_size(axis))]
    return lax.ppermute(value, axis, pairs)


def rate_logs():
    ranks = jnp.arange(RATES).astype(jnp.float32)
    return -0.0001 * jnp.power(jnp.float32(500.0), ranks / (RATES - 1))


def decay_parts(logrates, flags):
    length = flags.shape[0]
    sums = jnp.cumsum(logrates, axis=1)
    segment = jnp.cumsum(flags)
    order = jnp.arange(length)
    inside = (segment[:, None] == segment[None, :]) & (order[:, None] >= order[None, :])
    spread = sums[:, :, None] - sums[:, None, :]
    lower_mat = jnp.where(inside[None], jnp.exp(jnp.where(inside[None], spread, 0.0)), 0.0)
    cumulative = jnp.where((segment == 0)[None, :], jnp.exp(sums), 0.0)
    end_weight = lower_mat[:, length - 1, :]
    return (lower_mat, cumulative, end_weight)


def join_pairs(earlier, later):
    return (earlier[0] * later[0], later[0][:, None, None] * earlier[1] + later[1])


def pick_pair(flag, first, second):
    return (jnp.where(flag, first[0], second[0]), jnp.where(flag, first[1], second[1]))


def combine_levels(state, from_higher, bits):
    position = lax.axis_index("seq")
    prefix, total = state
    for bit in bits:
        other = partner(total, "seq", bit)
        high_half = position // (1 << bit) % 2 == 1
        takes_other = jnp.logical_not(high_half) if from_higher else high_half
        prefix = pick_pair(takes_other, join_pairs(other, prefix), prefix)
        total = pick_pair(takes_other, join_pairs(other, total), join_pairs(total, other))
    return prefix, total


def identity_pair(heads, shape):
    return (jnp.ones((heads,), jnp.float32), jnp.zeros((heads,) + shape, jnp.float32))


def chain_kernel(bits, shift, a_ref, e_ref, pa_ref, pe_ref, tot_a, tot_e, recv_a, recv_e, send_sem, recv_sem):
    seq_pos, dp_pos = lax.axis_index("seq"), lax.axis_index("dp")
    levels = len(bits)
    chains, groups = e_ref.shape[0], e_ref.shape[1]
    highs, partners = [], []
    for bit in bits:
        mask = 1 << bit
        up = seq_pos // mask % 2
        highs.append(up == 1)
        partners.append((dp_pos, seq_pos + mask - 2 * mask * up))
    barrier = pltpu.get_barrier_semaphore()
    for device in partners:
        pl.semaphore_signal(barrier, inc=1, device_id=device, device_id_type=MESH)
    pl.semaphore_wait(barrier, levels)
    pa_ref[...] = jnp.ones(pa_ref.shape, jnp.float32)
    pe_ref[...] = jnp.zeros(pe_ref.shape, jnp.float32)
    for slot in range(levels + shift * (groups - 1)):
        active = [(g, slot - shift * g) for g in range(groups) if 0 <= slot - shift * g < levels]
        work = []
        for g, lev in active:
            src_a = a_ref.at[g] if lev == 0 else tot_a.at[(lev - 1) % 2, g]
            src_e = [e_ref.at[c, g] if lev == 0 else tot_e.at[(lev - 1) % 2, c, g] for c in range(chains)]
            if lev == levels - 1:
                needed = highs[lev].astype(jnp.int32)
                source = e_ref.at[needed, g] if lev == 0 else tot_e.at[(lev - 1) % 2, needed, g]
                pairs = [(src_a, recv_a.at[lev, g]), (source, recv_e.at[lev, 0, g])]
            else:
                pairs = [(src_a, recv_a.at[lev, g])] + [(src_e[c], recv_e.at[lev, c, g]) for c in range(chains)]
            copies = []
            for k, (source, target) in enumerate(pairs):
                index = (lev * groups + g) * (chains + 1) + k
                copy = pltpu.make_async_remote_copy(
                    src_ref=source,
                    dst_ref=target,
                    send_sem=send_sem.at[index],
                    recv_sem=recv_sem.at[index],
                    device_id=partners[lev],
                    device_id_type=MESH,
                )
                copy.start()
                copies.append(copy)
            work.append((g, lev, src_a, src_e, copies))
        for g, lev, src_a, src_e, copies in work:
            for copy in copies:
                copy.wait()
            o_a = recv_a[lev, g]
            t_a = src_a[...]
            last = lev == levels - 1
            if not last:
                tot_a[lev % 2, g] = o_a * t_a
            for c in range(chains):
                takes = jnp.logical_not(highs[lev]) if c == 1 else highs[lev]
                o_e = recv_e[lev, 0 if last else c, g]
                p_a = pa_ref[c, g]
                p_e = pe_ref[c, g]
                pe_ref[c, g] = jnp.where(takes, p_a * o_e + p_e, p_e)
                pa_ref[c, g] = jnp.where(takes, o_a * p_a, p_a)
                if not last:
                    t_e = src_e[c][...]
                    tot_e[lev % 2, c, g] = jnp.where(takes, t_a * o_e + t_e, o_a * t_e + o_e)


def chip_scan(mines):
    heads = mines[0][0].shape[0]
    groups = 2
    quarter = heads // groups
    state, width = mines[0][1].shape[1:]
    rows = state * width // 128
    levels = lax.axis_size("seq").bit_length() - 1
    bits = tuple(range(1, levels))
    shift = (levels - 1) // 2
    a_in = jnp.broadcast_to(mines[0][0].reshape(groups, quarter, 1, 1), (groups, quarter, 1, 128))
    e_in = jnp.stack([mine[1].reshape(groups, quarter, rows, 128) for mine in mines])
    chains = len(mines)
    copies = len(bits) * groups * (chains + 1)
    pa, pe = pl.pallas_call(
        functools.partial(chain_kernel, bits, shift),
        out_shape=(
            jax.ShapeDtypeStruct((chains, groups, quarter, 1, 128), jnp.float32),
            jax.ShapeDtypeStruct((chains, groups, quarter, rows, 128), jnp.float32),
        ),
        in_specs=[pl.BlockSpec(memory_space=pltpu.VMEM)] * 2,
        out_specs=(pl.BlockSpec(memory_space=pltpu.VMEM), pl.BlockSpec(memory_space=pltpu.VMEM)),
        scratch_shapes=[
            pltpu.VMEM((2, groups, quarter, 1, 128), jnp.float32),
            pltpu.VMEM((2, chains, groups, quarter, rows, 128), jnp.float32),
            pltpu.VMEM((len(bits), groups, quarter, 1, 128), jnp.float32),
            pltpu.VMEM((len(bits), chains, groups, quarter, rows, 128), jnp.float32),
            pltpu.SemaphoreType.DMA((copies,)),
            pltpu.SemaphoreType.DMA((copies,)),
        ],
        compiler_params=pltpu.CompilerParams(collective_id=1, has_side_effects=True),
    )(a_in, e_in)
    return [(pa[c, :, :, 0, 0].reshape(heads), pe[c].reshape(heads, state, width)) for c in range(chains)]


def combine_chains(owns):
    heads = owns[0][0].shape[0]
    half = heads // 2
    shape = owns[0][1].shape[1:]
    core = lax.axis_index("seq") % 2
    directions = (False, True)
    in_chips, mines = [], []
    for own, from_higher in zip(owns, directions):
        in_chip, chip_total = combine_levels((identity_pair(heads, shape), own), from_higher, [0])
        in_chips.append(in_chip)
        mines.append(tuple(lax.dynamic_slice_in_dim(part, core * half, half, 0) for part in chip_total))
    results = []
    for across, in_chip in zip(chip_scan(mines), in_chips):
        sibling = partner(across, "seq", 0)
        low = pick_pair(core == 0, across, sibling)
        high = pick_pair(core == 0, sibling, across)
        full = tuple(jnp.concatenate([a, b], axis=0) for a, b in zip(low, high))
        results.append(join_pairs(full, in_chip))
    return results


def flat_bit_order(seq_bits, bits):
    near = [0, 1, 3, seq_bits + 1, 2, 4, seq_bits + 2, seq_bits, seq_bits + 3]
    order = []
    for b in near + list(range(bits)):
        if b < bits and b not in order:
            order.append(b)
    return order


def halving_kernel(seq_bits, order, buf_ref, out_ref, *scratch):
    steps = len(order)
    recvs = scratch[:steps]
    accs = scratch[steps:2 * steps - 1] + (out_ref,)
    send_sem, recv_sem = scratch[2 * steps - 1], scratch[2 * steps]
    stages = scratch[2 * steps + 1:]
    seq_pos, dp_pos = lax.axis_index("seq"), lax.axis_index("dp")
    targets = []
    for bit in order:
        if bit < seq_bits:
            mask = 1 << bit
            mine = seq_pos // mask % 2
            targets.append((mine, (dp_pos, seq_pos + mask - 2 * mask * mine)))
        else:
            mask = 1 << (bit - seq_bits)
            mine = dp_pos // mask % 2
            targets.append((mine, (dp_pos + mask - 2 * mask * mine, seq_pos)))
    barrier = pltpu.get_barrier_semaphore()
    for unused, device in targets:
        pl.semaphore_signal(barrier, inc=1, device_id=device, device_id_type=MESH)
    pl.semaphore_wait(barrier, steps)
    current = buf_ref
    staged = 0
    for step in range(steps):
        mine, device = targets[step]
        half = recvs[step].shape[0]
        if half % 8 == 0:
            source = current.at[pl.ds(pl.multiple_of((1 - mine) * half, 8), half)]
        else:
            source = stages[staged]
            staged += 1
            source[...] = jnp.where(mine == 1, current[0:half], current[half:2 * half])
        copy = pltpu.make_async_remote_copy(
            src_ref=source,
            dst_ref=recvs[step],
            send_sem=send_sem.at[step],
            recv_sem=recv_sem.at[step],
            device_id=device,
            device_id_type=MESH,
        )
        copy.start()
        if half % 8 == 0:
            keep = current[pl.ds(pl.multiple_of(mine * half, 8), half)]
        else:
            keep = jnp.where(mine == 1, current[half:2 * half], current[0:half])
        copy.wait()
        accs[step][...] = keep + recvs[step][...]
        current = accs[step]


def scatter_sum(product):
    dp_size, seq_size = lax.axis_size("dp"), lax.axis_size("seq")
    seq_bits = seq_size.bit_length() - 1
    bits = seq_bits + dp_size.bit_length() - 1
    rows, cols = product.shape
    block = rows // (dp_size * seq_size)
    order = flat_bit_order(seq_bits, bits)
    buf = product.reshape((2,) * bits + (block * cols,))
    buf = buf.transpose([bits - 1 - b for b in order] + [bits]).reshape(2**bits, block * cols)
    sizes = [2 ** (bits - 1 - step) for step in range(bits)]
    scratch = [pltpu.VMEM((size, block * cols), jnp.float32) for size in sizes]
    scratch += [pltpu.VMEM((size, block * cols), jnp.float32) for size in sizes[:-1]]
    scratch += [pltpu.SemaphoreType.DMA((bits,)), pltpu.SemaphoreType.DMA((bits,))]
    scratch += [pltpu.VMEM((size, block * cols), jnp.float32) for size in sizes if size % 8]
    out = pl.pallas_call(
        functools.partial(halving_kernel, seq_bits, order),
        out_shape=jax.ShapeDtypeStruct((1, block * cols), jnp.float32),
        in_specs=[pl.BlockSpec(memory_space=pltpu.VMEM)],
        out_specs=pl.BlockSpec(memory_space=pltpu.VMEM),
        scratch_shapes=scratch,
        compiler_params=pltpu.CompilerParams(collective_id=0, has_side_effects=True),
    )(buf)
    return out.reshape(block, cols)


def local(normed, values, cotangent, w_bc, rate_index, starts):
    hidden = normed[0]
    length = hidden.shape[0]
    heads = rate_index.shape[1]
    width = values.shape[2]
    head_dim = width // heads
    state = w_bc.shape[1] // 2
    proj = jnp.dot(hidden, w_bc, preferred_element_type=jnp.float32).astype(jnp.bfloat16)
    bmat = proj[:, :state].astype(jnp.float32)
    cmat = proj[:, state:].astype(jnp.float32)
    levels_table = rate_logs()
    matches = rate_index[0][:, :, None] == jnp.arange(RATES)[None, None, :]
    logrates = jnp.sum(jnp.where(matches, levels_table[None, None, :], 0.0), axis=2)
    lower_mat, cumulative, end_weight = decay_parts(logrates, starts[0])
    vals = values[0].astype(jnp.float32).reshape(length, heads, head_dim)
    cots = cotangent[0].astype(jnp.float32).reshape(length, heads, head_dim)
    decay_total = cumulative[:, -1]
    ends = jnp.einsum("hk,kn,khp->hnp", end_weight, bmat, vals, precision=highest)
    feeds = jnp.einsum("hk,kn,khp->hnp", cumulative, cmat, cots, precision=highest)
    before_pair, after_pair = combine_chains([(decay_total, ends), (decay_total, feeds)])
    before, after = before_pair[1], after_pair[1]
    scores = jnp.dot(cmat, bmat.T, precision=highest)
    mixed = lower_mat * scores[None]
    grad_vals = jnp.einsum("hts,thp->shp", mixed, cots, precision=highest)
    grad_vals = grad_vals + end_weight.T[:, :, None] * jnp.einsum(
        "sn,hnp->shp", bmat, after, precision=highest
    )
    paired = lower_mat * jnp.einsum("thp,shp->hts", cots, vals, precision=highest)
    grad_b = jnp.einsum("hts,tn->sn", paired, cmat, precision=highest)
    grad_b = grad_b + jnp.einsum("hs,shp,hnp->sn", end_weight, vals, after, precision=highest)
    grad_c = jnp.einsum("hts,sn->tn", paired, bmat, precision=highest)
    grad_c = grad_c + jnp.einsum("ht,thp,hnp->tn", cumulative, cots, before, precision=highest)
    grad_values = grad_vals.reshape(length, width).astype(jnp.bfloat16)[None]
    grad_bc = jnp.concatenate([grad_b, grad_c], axis=1).astype(jnp.bfloat16)
    scale = 1.0 / (lax.axis_size("dp") * lax.axis_size("seq") * length)
    product = lax.dot_general(
        hidden, grad_bc, (((0,), (0,)), ((), ())), preferred_element_type=jnp.float32
    )
    grad_wbc = scatter_sum(product) * scale
    return (grad_values, grad_wbc)


def solution(mesh):
    placed = (
        P("dp", "seq", None),
        P("dp", "seq", None),
        P("dp", "seq", None),
        P(),
        P("dp", None, "seq"),
        P("dp", "seq"),
    )
    return jax.shard_map(
        local,
        mesh=mesh,
        in_specs=placed,
        out_specs=(P("dp", "seq", None), P(("dp", "seq"), None)),
        check_vma=False,
    )
```

```python
import functools

import jax
import jax.numpy as jnp
from jax import lax
from jax.experimental import pallas as pl
from jax.experimental.pallas import tpu as pltpu
from jax.sharding import PartitionSpec as P

MESH = pl.DeviceIdType.MESH

RATES = 16


highest = lax.Precision.HIGHEST


def partner(value, axis, apart):
    mask = 2**apart
    pairs = [(source, source ^ mask) for source in range(lax.axis_size(axis))]
    return lax.ppermute(value, axis, pairs)


def rate_logs():
    ranks = jnp.arange(RATES).astype(jnp.float32)
    return -0.0001 * jnp.power(jnp.float32(500.0), ranks / (RATES - 1))


def decay_parts(logrates, flags):
    length = flags.shape[0]
    sums = jnp.cumsum(logrates, axis=1)
    segment = jnp.cumsum(flags)
    order = jnp.arange(length)
    inside = (segment[:, None] == segment[None, :]) & (order[:, None] >= order[None, :])
    spread = sums[:, :, None] - sums[:, None, :]
    lower_mat = jnp.where(inside[None], jnp.exp(jnp.where(inside[None], spread, 0.0)), 0.0)
    cumulative = jnp.where((segment == 0)[None, :], jnp.exp(sums), 0.0)
    end_weight = lower_mat[:, length - 1, :]
    return (lower_mat, cumulative, end_weight)


def join_pairs(earlier, later):
    return (earlier[0] * later[0], later[0][:, None, None] * earlier[1] + later[1])


def pick_pair(flag, first, second):
    return (jnp.where(flag, first[0], second[0]), jnp.where(flag, first[1], second[1]))


def combine_levels(state, from_higher, bits):
    position = lax.axis_index("seq")
    prefix, total = state
    for bit in bits:
        other = partner(total, "seq", bit)
        high_half = position // (1 << bit) % 2 == 1
        takes_other = jnp.logical_not(high_half) if from_higher else high_half
        prefix = pick_pair(takes_other, join_pairs(other, prefix), prefix)
        total = pick_pair(takes_other, join_pairs(other, total), join_pairs(total, other))
    return prefix, total


def identity_pair(heads, shape):
    return (jnp.ones((heads,), jnp.float32), jnp.zeros((heads,) + shape, jnp.float32))


def chain_kernel(bits, shift, a_ref, es_ref, eg_ref, pa_ref, pes_ref, peg_ref, tot_a, tot_e, recv_a, recv_e, send_sem, recv_sem):
    e_refs, pe_refs = (es_ref, eg_ref), (pes_ref, peg_ref)
    seq_pos, dp_pos = lax.axis_index("seq"), lax.axis_index("dp")
    levels = len(bits)
    chains, groups = len(e_refs), es_ref.shape[0]
    highs, partners = [], []
    for bit in bits:
        mask = 1 << bit
        up = seq_pos // mask % 2
        highs.append(up == 1)
        partners.append((dp_pos, seq_pos + mask - 2 * mask * up))
    barrier = pltpu.get_barrier_semaphore()
    for device in partners:
        pl.semaphore_signal(barrier, inc=1, device_id=device, device_id_type=MESH)
    pl.semaphore_wait(barrier, levels)
    pa_ref[...] = jnp.ones(pa_ref.shape, jnp.float32)
    for pe_ref in pe_refs:
        pe_ref[...] = jnp.zeros(pe_ref.shape, jnp.float32)
    for slot in range(levels + shift * (groups - 1)):
        active = [(g, slot - shift * g) for g in range(groups) if 0 <= slot - shift * g < levels]
        work = []
        for g, lev in active:
            src_a = a_ref.at[g] if lev == 0 else tot_a.at[(lev - 1) % 2, g]
            src_e = [e_refs[c].at[g] if lev == 0 else tot_e.at[(lev - 1) % 2, c, g] for c in range(chains)]
            if lev == levels - 1:
                needed = highs[lev].astype(jnp.int32)
                source = tot_e.at[(lev - 1) % 2, needed, g]
                pairs = [(src_a, recv_a.at[lev, g]), (source, recv_e.at[lev, 0, g])]
            else:
                pairs = [(src_a, recv_a.at[lev, g])] + [(src_e[c], recv_e.at[lev, c, g]) for c in range(chains)]
            copies = []
            for k, (source, target) in enumerate(pairs):
                index = (lev * groups + g) * (chains + 1) + k
                copy = pltpu.make_async_remote_copy(
                    src_ref=source,
                    dst_ref=target,
                    send_sem=send_sem.at[index],
                    recv_sem=recv_sem.at[index],
                    device_id=partners[lev],
                    device_id_type=MESH,
                )
                copy.start()
                copies.append(copy)
            work.append((g, lev, src_a, src_e, copies))
        for g, lev, src_a, src_e, copies in work:
            for copy in copies:
                copy.wait()
            o_a = recv_a[lev, g]
            t_a = src_a[...]
            last = lev == levels - 1
            if not last:
                tot_a[lev % 2, g] = o_a * t_a
            for c in range(chains):
                takes = jnp.logical_not(highs[lev]) if c == 1 else highs[lev]
                o_e = recv_e[lev, 0 if last else c, g]
                p_a = pa_ref[c, g]
                p_e = pe_refs[c][g]
                pe_refs[c][g] = jnp.where(takes, p_a * o_e + p_e, p_e)
                pa_ref[c, g] = jnp.where(takes, o_a * p_a, p_a)
                if not last:
                    t_e = src_e[c][...]
                    tot_e[lev % 2, c, g] = jnp.where(takes, t_a * o_e + t_e, o_a * t_e + o_e)


def chip_scan(mines):
    heads = mines[0][0].shape[0]
    groups = 2
    quarter = heads // groups
    state, width = mines[0][1].shape[1:]
    rows = state * width // 128
    levels = lax.axis_size("seq").bit_length() - 1
    bits = tuple(range(1, levels))
    shift = (levels - 1) // 2
    a_in = jnp.broadcast_to(mines[0][0].reshape(groups, quarter, 1, 1), (groups, quarter, 1, 128))
    e_in = [mine[1].reshape(groups, quarter, rows, 128) for mine in mines]
    chains = len(mines)
    copies = len(bits) * groups * (chains + 1)
    vmem = pl.BlockSpec(memory_space=pltpu.VMEM)
    pa, pes, peg = pl.pallas_call(
        functools.partial(chain_kernel, bits, shift),
        out_shape=(
            jax.ShapeDtypeStruct((chains, groups, quarter, 1, 128), jnp.float32),
            jax.ShapeDtypeStruct((groups, quarter, rows, 128), jnp.float32),
            jax.ShapeDtypeStruct((groups, quarter, rows, 128), jnp.float32),
        ),
        in_specs=[vmem] * 3,
        out_specs=(vmem, vmem, vmem),
        scratch_shapes=[
            pltpu.VMEM((2, groups, quarter, 1, 128), jnp.float32),
            pltpu.VMEM((2, chains, groups, quarter, rows, 128), jnp.float32),
            pltpu.VMEM((len(bits), groups, quarter, 1, 128), jnp.float32),
            pltpu.VMEM((len(bits), chains, groups, quarter, rows, 128), jnp.float32),
            pltpu.SemaphoreType.DMA((copies,)),
            pltpu.SemaphoreType.DMA((copies,)),
        ],
        compiler_params=pltpu.CompilerParams(collective_id=1, has_side_effects=True),
    )(a_in, *e_in)
    return [(pa[c, :, :, 0, 0].reshape(heads), pe.reshape(heads, state, width)) for c, pe in enumerate((pes, peg))]


def combine_chains(owns):
    heads = owns[0][0].shape[0]
    half = heads // 2
    shape = owns[0][1].shape[1:]
    core = lax.axis_index("seq") % 2
    directions = (False, True)
    in_chips, mines = [], []
    for own, from_higher in zip(owns, directions):
        in_chip, chip_total = combine_levels((identity_pair(heads, shape), own), from_higher, [0])
        in_chips.append(in_chip)
        mines.append(tuple(lax.dynamic_slice_in_dim(part, core * half, half, 0) for part in chip_total))
    results = []
    for across, in_chip in zip(chip_scan(mines), in_chips):
        sibling = partner(across, "seq", 0)
        low = pick_pair(core == 0, across, sibling)
        high = pick_pair(core == 0, sibling, across)
        full = tuple(jnp.concatenate([a, b], axis=0) for a, b in zip(low, high))
        results.append(join_pairs(full, in_chip))
    return results


def flat_bit_order(seq_bits, bits):
    near = [0, 1, 3, seq_bits + 1, 2, 4, seq_bits + 2, seq_bits, seq_bits + 3]
    order = []
    for b in near + list(range(bits)):
        if b < bits and b not in order:
            order.append(b)
    return order


def halving_kernel(seq_bits, order, buf_ref, out_ref, *scratch):
    steps = len(order)
    recvs = scratch[:steps]
    accs = scratch[steps:2 * steps - 1] + (out_ref,)
    send_sem, recv_sem = scratch[2 * steps - 1], scratch[2 * steps]
    stages = scratch[2 * steps + 1:]
    seq_pos, dp_pos = lax.axis_index("seq"), lax.axis_index("dp")
    targets = []
    for bit in order:
        if bit < seq_bits:
            mask = 1 << bit
            mine = seq_pos // mask % 2
            targets.append((mine, (dp_pos, seq_pos + mask - 2 * mask * mine)))
        else:
            mask = 1 << (bit - seq_bits)
            mine = dp_pos // mask % 2
            targets.append((mine, (dp_pos + mask - 2 * mask * mine, seq_pos)))
    barrier = pltpu.get_barrier_semaphore()
    for unused, device in targets:
        pl.semaphore_signal(barrier, inc=1, device_id=device, device_id_type=MESH)
    pl.semaphore_wait(barrier, steps)
    current = buf_ref
    staged = 0
    for step in range(steps):
        mine, device = targets[step]
        half = recvs[step].shape[0]
        if half % 8 == 0:
            source = current.at[pl.ds(pl.multiple_of((1 - mine) * half, 8), half)]
        else:
            source = stages[staged]
            staged += 1
            source[...] = jnp.where(mine == 1, current[0:half], current[half:2 * half])
        copy = pltpu.make_async_remote_copy(
            src_ref=source,
            dst_ref=recvs[step],
            send_sem=send_sem.at[step],
            recv_sem=recv_sem.at[step],
            device_id=device,
            device_id_type=MESH,
        )
        copy.start()
        if half % 8 == 0:
            keep = current[pl.ds(pl.multiple_of(mine * half, 8), half)]
        else:
            keep = jnp.where(mine == 1, current[half:2 * half], current[0:half])
        copy.wait()
        accs[step][...] = keep + recvs[step][...]
        current = accs[step]


def scatter_sum(product):
    dp_size, seq_size = lax.axis_size("dp"), lax.axis_size("seq")
    seq_bits = seq_size.bit_length() - 1
    bits = seq_bits + dp_size.bit_length() - 1
    rows, cols = product.shape
    block = rows // (dp_size * seq_size)
    order = flat_bit_order(seq_bits, bits)
    buf = product.reshape((2,) * bits + (block * cols,))
    buf = buf.transpose([bits - 1 - b for b in order] + [bits]).reshape(2**bits, block * cols)
    sizes = [2 ** (bits - 1 - step) for step in range(bits)]
    scratch = [pltpu.VMEM((size, block * cols), jnp.float32) for size in sizes]
    scratch += [pltpu.VMEM((size, block * cols), jnp.float32) for size in sizes[:-1]]
    scratch += [pltpu.SemaphoreType.DMA((bits,)), pltpu.SemaphoreType.DMA((bits,))]
    scratch += [pltpu.VMEM((size, block * cols), jnp.float32) for size in sizes if size % 8]
    out = pl.pallas_call(
        functools.partial(halving_kernel, seq_bits, order),
        out_shape=jax.ShapeDtypeStruct((1, block * cols), jnp.float32),
        in_specs=[pl.BlockSpec(memory_space=pltpu.VMEM)],
        out_specs=pl.BlockSpec(memory_space=pltpu.VMEM),
        scratch_shapes=scratch,
        compiler_params=pltpu.CompilerParams(collective_id=0, has_side_effects=True),
    )(buf)
    return out.reshape(block, cols)


def local(normed, values, cotangent, w_bc, rate_index, starts):
    hidden = normed[0]
    length = hidden.shape[0]
    heads = rate_index.shape[1]
    width = values.shape[2]
    head_dim = width // heads
    state = w_bc.shape[1] // 2
    proj = jnp.dot(hidden, w_bc, preferred_element_type=jnp.float32).astype(jnp.bfloat16)
    bmat = proj[:, :state].astype(jnp.float32)
    cmat = proj[:, state:].astype(jnp.float32)
    levels_table = rate_logs()
    matches = rate_index[0][:, :, None] == jnp.arange(RATES)[None, None, :]
    logrates = jnp.sum(jnp.where(matches, levels_table[None, None, :], 0.0), axis=2)
    lower_mat, cumulative, end_weight = decay_parts(logrates, starts[0])
    vals = values[0].astype(jnp.float32).reshape(length, heads, head_dim)
    cots = cotangent[0].astype(jnp.float32).reshape(length, heads, head_dim)
    decay_total = cumulative[:, -1]
    ends = jnp.einsum("hk,kn,khp->hpn", end_weight, bmat, vals, precision=highest)
    feeds = jnp.einsum("hk,kn,khp->hpn", cumulative, cmat, cots, precision=highest)
    before_pair, after_pair = combine_chains([(decay_total, ends), (decay_total, feeds)])
    before, after = before_pair[1], after_pair[1]
    scores = jnp.dot(cmat, bmat.T, precision=highest)
    mixed = lower_mat * scores[None]
    grad_vals = jnp.einsum("hts,thp->shp", mixed, cots, precision=highest)
    grad_vals = grad_vals + end_weight.T[:, :, None] * jnp.einsum(
        "sn,hpn->shp", bmat, after, precision=highest
    )
    paired = lower_mat * jnp.einsum("thp,shp->hts", cots, vals, precision=highest)
    grad_b = jnp.einsum("hts,tn->sn", paired, cmat, precision=highest)
    grad_b = grad_b + jnp.einsum("hs,shp,hpn->sn", end_weight, vals, after, precision=highest)
    grad_c = jnp.einsum("hts,sn->tn", paired, bmat, precision=highest)
    grad_c = grad_c + jnp.einsum("ht,thp,hpn->tn", cumulative, cots, before, precision=highest)
    grad_values = grad_vals.reshape(length, width).astype(jnp.bfloat16)[None]
    grad_bc = jnp.concatenate([grad_b, grad_c], axis=1).astype(jnp.bfloat16)
    scale = 1.0 / (lax.axis_size("dp") * lax.axis_size("seq") * length)
    product = lax.dot_general(
        hidden, grad_bc, (((0,), (0,)), ((), ())), preferred_element_type=jnp.float32
    )
    grad_wbc = scatter_sum(product) * scale
    return (grad_values, grad_wbc)


def solution(mesh):
    placed = (
        P("dp", "seq", None),
        P("dp", "seq", None),
        P("dp", "seq", None),
        P(),
        P("dp", None, "seq"),
        P("dp", "seq"),
    )
    return jax.shard_map(
        local,
        mesh=mesh,
        in_specs=placed,
        out_specs=(P("dp", "seq", None), P(("dp", "seq"), None)),
        check_vma=False,
    )
```

```python
import functools

import jax
import jax.numpy as jnp
from jax import lax
from jax.experimental import pallas as pl
from jax.experimental.pallas import tpu as pltpu
from jax.sharding import PartitionSpec as P

MESH = pl.DeviceIdType.MESH

RATES = 16


highest = lax.Precision.HIGHEST


def partner(value, axis, apart):
    mask = 2**apart
    pairs = [(source, source ^ mask) for source in range(lax.axis_size(axis))]
    return lax.ppermute(value, axis, pairs)


def rate_logs():
    ranks = jnp.arange(RATES).astype(jnp.float32)
    return -0.0001 * jnp.power(jnp.float32(500.0), ranks / (RATES - 1))


def decay_parts(logrates, flags):
    length = flags.shape[0]
    sums = jnp.cumsum(logrates, axis=1)
    segment = jnp.cumsum(flags)
    order = jnp.arange(length)
    inside = (segment[:, None] == segment[None, :]) & (order[:, None] >= order[None, :])
    spread = sums[:, :, None] - sums[:, None, :]
    lower_mat = jnp.where(inside[None], jnp.exp(jnp.where(inside[None], spread, 0.0)), 0.0)
    cumulative = jnp.where((segment == 0)[None, :], jnp.exp(sums), 0.0)
    end_weight = lower_mat[:, length - 1, :]
    return (lower_mat, cumulative, end_weight)


def join_pairs(earlier, later):
    return (earlier[0] * later[0], later[0][:, None, None] * earlier[1] + later[1])


def pick_pair(flag, first, second):
    return (jnp.where(flag, first[0], second[0]), jnp.where(flag, first[1], second[1]))


def combine_levels(state, from_higher, bits):
    position = lax.axis_index("seq")
    prefix, total = state
    for bit in bits:
        other = partner(total, "seq", bit)
        high_half = position // (1 << bit) % 2 == 1
        takes_other = jnp.logical_not(high_half) if from_higher else high_half
        prefix = pick_pair(takes_other, join_pairs(other, prefix), prefix)
        total = pick_pair(takes_other, join_pairs(other, total), join_pairs(total, other))
    return prefix, total


def identity_pair(heads, shape):
    return (jnp.ones((heads,), jnp.float32), jnp.zeros((heads,) + shape, jnp.float32))


def chain_kernel(bits, shift, a_ref, es_ref, eg_ref, pa_ref, pes_ref, peg_ref, tot_a, tot_e, recv_a, recv_e, send_sem, recv_sem):
    e_refs, pe_refs = (es_ref, eg_ref), (pes_ref, peg_ref)
    seq_pos, dp_pos = lax.axis_index("seq"), lax.axis_index("dp")
    levels = len(bits)
    chains, groups = len(e_refs), es_ref.shape[0]
    highs, partners = [], []
    for bit in bits:
        mask = 1 << bit
        up = seq_pos // mask % 2
        highs.append(up == 1)
        partners.append((dp_pos, seq_pos + mask - 2 * mask * up))
    barrier = pltpu.get_barrier_semaphore()
    for device in partners:
        pl.semaphore_signal(barrier, inc=1, device_id=device, device_id_type=MESH)
    pl.semaphore_wait(barrier, levels)
    pa_ref[...] = jnp.ones(pa_ref.shape, jnp.float32)
    for pe_ref in pe_refs:
        pe_ref[...] = jnp.zeros(pe_ref.shape, jnp.float32)
    for slot in range(levels + shift * (groups - 1)):
        active = [(g, slot - shift * g) for g in range(groups) if 0 <= slot - shift * g < levels]
        work = []
        for g, lev in active:
            src_a = a_ref.at[g] if lev == 0 else tot_a.at[(lev - 1) % 2, g]
            src_e = [e_refs[c].at[g] if lev == 0 else tot_e.at[(lev - 1) % 2, c, g] for c in range(chains)]
            if lev == levels - 1:
                needed = highs[lev].astype(jnp.int32)
                source = tot_e.at[(lev - 1) % 2, needed, g]
                pairs = [(src_a, recv_a.at[lev, g]), (source, recv_e.at[lev, 0, g])]
            else:
                pairs = [(src_a, recv_a.at[lev, g])] + [(src_e[c], recv_e.at[lev, c, g]) for c in range(chains)]
            copies = []
            for k, (source, target) in enumerate(pairs):
                index = (lev * groups + g) * (chains + 1) + k
                copy = pltpu.make_async_remote_copy(
                    src_ref=source,
                    dst_ref=target,
                    send_sem=send_sem.at[index],
                    recv_sem=recv_sem.at[index],
                    device_id=partners[lev],
                    device_id_type=MESH,
                )
                copy.start()
                copies.append(copy)
            work.append((g, lev, src_a, src_e, copies))
        for g, lev, src_a, src_e, copies in work:
            for copy in copies:
                copy.wait()
            o_a = recv_a[lev, g]
            t_a = src_a[...]
            last = lev == levels - 1
            if not last:
                tot_a[lev % 2, g] = o_a * t_a
            for c in range(chains):
                takes = jnp.logical_not(highs[lev]) if c == 1 else highs[lev]
                o_e = recv_e[lev, 0 if last else c, g]
                p_a = pa_ref[c, g]
                p_e = pe_refs[c][g]
                pe_refs[c][g] = jnp.where(takes, p_a * o_e + p_e, p_e)
                pa_ref[c, g] = jnp.where(takes, o_a * p_a, p_a)
                if not last:
                    t_e = src_e[c][...]
                    tot_e[lev % 2, c, g] = jnp.where(takes, t_a * o_e + t_e, o_a * t_e + o_e)


def chip_scan(mines):
    heads = mines[0][0].shape[0]
    groups = 2
    quarter = heads // groups
    state, width = mines[0][1].shape[1:]
    rows = state * width // 128
    levels = lax.axis_size("seq").bit_length() - 1
    bits = tuple(range(1, levels))
    shift = (levels - 1) // 2
    a_in = jnp.broadcast_to(mines[0][0].reshape(groups, quarter, 1, 1), (groups, quarter, 1, 128))
    e_in = [mine[1].reshape(groups, quarter, rows, 128) for mine in mines]
    chains = len(mines)
    copies = len(bits) * groups * (chains + 1)
    vmem = pl.BlockSpec(memory_space=pltpu.VMEM)
    pa, pes, peg = pl.pallas_call(
        functools.partial(chain_kernel, bits, shift),
        out_shape=(
            jax.ShapeDtypeStruct((chains, groups, quarter, 1, 128), jnp.float32),
            jax.ShapeDtypeStruct((groups, quarter, rows, 128), jnp.float32),
            jax.ShapeDtypeStruct((groups, quarter, rows, 128), jnp.float32),
        ),
        in_specs=[vmem] * 3,
        out_specs=(vmem, vmem, vmem),
        scratch_shapes=[
            pltpu.VMEM((2, groups, quarter, 1, 128), jnp.float32),
            pltpu.VMEM((2, chains, groups, quarter, rows, 128), jnp.float32),
            pltpu.VMEM((len(bits), groups, quarter, 1, 128), jnp.float32),
            pltpu.VMEM((len(bits), chains, groups, quarter, rows, 128), jnp.float32),
            pltpu.SemaphoreType.DMA((copies,)),
            pltpu.SemaphoreType.DMA((copies,)),
        ],
        compiler_params=pltpu.CompilerParams(collective_id=1, has_side_effects=True),
    )(a_in, *e_in)
    return [(pa[c, :, :, 0, 0].reshape(heads), pe.reshape(heads, state, width)) for c, pe in enumerate((pes, peg))]


def combine_chains(owns):
    heads = owns[0][0].shape[0]
    half = heads // 2
    shape = owns[0][1].shape[1:]
    core = lax.axis_index("seq") % 2
    directions = (False, True)
    in_chips, mines = [], []
    for own, from_higher in zip(owns, directions):
        in_chip, chip_total = combine_levels((identity_pair(heads, shape), own), from_higher, [0])
        in_chips.append(in_chip)
        mines.append(tuple(lax.dynamic_slice_in_dim(part, core * half, half, 0) for part in chip_total))
    results = []
    for across, in_chip in zip(chip_scan(mines), in_chips):
        sibling = partner(across, "seq", 0)
        low = pick_pair(core == 0, across, sibling)
        high = pick_pair(core == 0, sibling, across)
        full = tuple(jnp.concatenate([a, b], axis=0) for a, b in zip(low, high))
        results.append(join_pairs(full, in_chip))
    return results


def flat_bit_order(seq_bits, bits, near):
    order = []
    for b in near + list(range(bits)):
        if b < bits and b not in order:
            order.append(b)
    return order


def halving_kernel(seq_bits, orders, *refs):
    lanes = len(orders)
    steps = len(orders[0])
    bufs, outs, scratch = refs[:lanes], refs[lanes:2 * lanes], refs[2 * lanes:]
    small = sum(1 for step in range(steps) if (2 ** (steps - 1 - step)) % 8)
    per_lane = steps + steps - 1 + small
    send_sem, recv_sem = scratch[lanes * per_lane], scratch[lanes * per_lane + 1]
    seq_pos, dp_pos = lax.axis_index("seq"), lax.axis_index("dp")
    targets = {}
    for bit in range(steps):
        if bit < seq_bits:
            mask = 1 << bit
            mine = seq_pos // mask % 2
            targets[bit] = (mine, (dp_pos, seq_pos + mask - 2 * mask * mine))
        else:
            mask = 1 << (bit - seq_bits)
            mine = dp_pos // mask % 2
            targets[bit] = (mine, (dp_pos + mask - 2 * mask * mine, seq_pos))
    barrier = pltpu.get_barrier_semaphore()
    for bit in range(steps):
        pl.semaphore_signal(barrier, inc=1, device_id=targets[bit][1], device_id_type=MESH)
    pl.semaphore_wait(barrier, steps)
    currents = list(bufs)
    for step in range(steps):
        pending = []
        for lane in range(lanes):
            base = scratch[lane * per_lane:(lane + 1) * per_lane]
            recvs, accs, stages = base[:steps], base[steps:2 * steps - 1] + (outs[lane],), base[2 * steps - 1:]
            mine, device = targets[orders[lane][step]]
            current = currents[lane]
            half = recvs[step].shape[0]
            if half % 8 == 0:
                source = current.at[pl.ds(pl.multiple_of((1 - mine) * half, 8), half)]
            else:
                source = stages[step - (steps - small)]
                source[...] = jnp.where(mine == 1, current[0:half], current[half:2 * half])
            copy = pltpu.make_async_remote_copy(
                src_ref=source,
                dst_ref=recvs[step],
                send_sem=send_sem.at[lane * steps + step],
                recv_sem=recv_sem.at[lane * steps + step],
                device_id=device,
                device_id_type=MESH,
            )
            copy.start()
            pending.append((lane, copy, mine, half, current, recvs[step], accs[step]))
        for lane, copy, mine, half, current, received, acc in pending:
            if half % 8 == 0:
                keep = current[pl.ds(pl.multiple_of(mine * half, 8), half)]
            else:
                keep = jnp.where(mine == 1, current[half:2 * half], current[0:half])
            copy.wait()
            acc[...] = keep + received[...]
            currents[lane] = acc


def scatter_sum(product):
    dp_size, seq_size = lax.axis_size("dp"), lax.axis_size("seq")
    seq_bits = seq_size.bit_length() - 1
    bits = seq_bits + dp_size.bit_length() - 1
    rows, cols = product.shape
    block = rows // (dp_size * seq_size)
    s = seq_bits
    orders = [
        flat_bit_order(s, bits, [0, 1, 3, s + 1, 2, 4, s + 2, s, s + 3]),
        flat_bit_order(s, bits, [0, 3, s + 1, 1, 4, s + 2, 2, s, s + 3]),
    ]
    lanes = len(orders)
    width = cols // lanes
    bufs = []
    for lane, order in enumerate(orders):
        part = product[:, lane * width:(lane + 1) * width].reshape((2,) * bits + (block * width,))
        part = part.transpose([bits - 1 - b for b in order] + [bits]).reshape(2**bits, block * width)
        bufs.append(part)
    sizes = [2 ** (bits - 1 - step) for step in range(bits)]
    scratch = []
    for lane in range(lanes):
        scratch += [pltpu.VMEM((size, block * width), jnp.float32) for size in sizes]
        scratch += [pltpu.VMEM((size, block * width), jnp.float32) for size in sizes[:-1]]
        scratch += [pltpu.VMEM((size, block * width), jnp.float32) for size in sizes if size % 8]
    scratch += [pltpu.SemaphoreType.DMA((lanes * bits,)), pltpu.SemaphoreType.DMA((lanes * bits,))]
    vmem = pl.BlockSpec(memory_space=pltpu.VMEM)
    outs = pl.pallas_call(
        functools.partial(halving_kernel, seq_bits, orders),
        out_shape=tuple(jax.ShapeDtypeStruct((1, block * width), jnp.float32) for _ in orders),
        in_specs=[vmem] * lanes,
        out_specs=tuple(vmem for _ in orders),
        scratch_shapes=scratch,
        compiler_params=pltpu.CompilerParams(collective_id=0, has_side_effects=True),
    )(*bufs)
    return jnp.concatenate([out.reshape(block, width) for out in outs], axis=1)


def local(normed, values, cotangent, w_bc, rate_index, starts):
    hidden = normed[0]
    length = hidden.shape[0]
    heads = rate_index.shape[1]
    width = values.shape[2]
    head_dim = width // heads
    state = w_bc.shape[1] // 2
    proj = jnp.dot(hidden, w_bc, preferred_element_type=jnp.float32).astype(jnp.bfloat16)
    bmat = proj[:, :state].astype(jnp.float32)
    cmat = proj[:, state:].astype(jnp.float32)
    levels_table = rate_logs()
    matches = rate_index[0][:, :, None] == jnp.arange(RATES)[None, None, :]
    logrates = jnp.sum(jnp.where(matches, levels_table[None, None, :], 0.0), axis=2)
    lower_mat, cumulative, end_weight = decay_parts(logrates, starts[0])
    vals = values[0].astype(jnp.float32).reshape(length, heads, head_dim)
    cots = cotangent[0].astype(jnp.float32).reshape(length, heads, head_dim)
    decay_total = cumulative[:, -1]
    ends = jnp.einsum("hk,kn,khp->hpn", end_weight, bmat, vals, precision=highest)
    feeds = jnp.einsum("hk,kn,khp->hpn", cumulative, cmat, cots, precision=highest)
    before_pair, after_pair = combine_chains([(decay_total, ends), (decay_total, feeds)])
    before, after = before_pair[1], after_pair[1]
    scores = jnp.dot(cmat, bmat.T, precision=highest)
    mixed = lower_mat * scores[None]
    grad_vals = jnp.einsum("hts,thp->shp", mixed, cots, precision=highest)
    grad_vals = grad_vals + end_weight.T[:, :, None] * jnp.einsum(
        "sn,hpn->shp", bmat, after, precision=highest
    )
    paired = lower_mat * jnp.einsum("thp,shp->hts", cots, vals, precision=highest)
    grad_b = jnp.einsum("hts,tn->sn", paired, cmat, precision=highest)
    grad_b = grad_b + jnp.einsum("hs,shp,hpn->sn", end_weight, vals, after, precision=highest)
    grad_c = jnp.einsum("hts,sn->tn", paired, bmat, precision=highest)
    grad_c = grad_c + jnp.einsum("ht,thp,hpn->tn", cumulative, cots, before, precision=highest)
    grad_values = grad_vals.reshape(length, width).astype(jnp.bfloat16)[None]
    grad_bc = jnp.concatenate([grad_b, grad_c], axis=1).astype(jnp.bfloat16)
    scale = 1.0 / (lax.axis_size("dp") * lax.axis_size("seq") * length)
    product = lax.dot_general(
        hidden, grad_bc, (((0,), (0,)), ((), ())), preferred_element_type=jnp.float32
    )
    grad_wbc = scatter_sum(product) * scale
    return (grad_values, grad_wbc)


def solution(mesh):
    placed = (
        P("dp", "seq", None),
        P("dp", "seq", None),
        P("dp", "seq", None),
        P(),
        P("dp", None, "seq"),
        P("dp", "seq"),
    )
    return jax.shard_map(
        local,
        mesh=mesh,
        in_specs=placed,
        out_specs=(P("dp", "seq", None), P(("dp", "seq"), None)),
        check_vma=False,
    )
```

```python
import functools

import jax
import jax.numpy as jnp
from jax import lax
from jax.experimental import pallas as pl
from jax.experimental.pallas import tpu as pltpu
from jax.sharding import PartitionSpec as P

MESH = pl.DeviceIdType.MESH

RATES = 16


highest = lax.Precision.HIGHEST


def partner(value, axis, apart):
    mask = 2**apart
    pairs = [(source, source ^ mask) for source in range(lax.axis_size(axis))]
    return lax.ppermute(value, axis, pairs)


def rate_logs():
    ranks = jnp.arange(RATES).astype(jnp.float32)
    return -0.0001 * jnp.power(jnp.float32(500.0), ranks / (RATES - 1))


def decay_parts(logrates, flags):
    length = flags.shape[0]
    sums = jnp.cumsum(logrates, axis=1)
    segment = jnp.cumsum(flags)
    order = jnp.arange(length)
    inside = (segment[:, None] == segment[None, :]) & (order[:, None] >= order[None, :])
    spread = sums[:, :, None] - sums[:, None, :]
    lower_mat = jnp.where(inside[None], jnp.exp(jnp.where(inside[None], spread, 0.0)), 0.0)
    cumulative = jnp.where((segment == 0)[None, :], jnp.exp(sums), 0.0)
    end_weight = lower_mat[:, length - 1, :]
    return (lower_mat, cumulative, end_weight)


def join_pairs(earlier, later):
    return (earlier[0] * later[0], later[0][:, None, None] * earlier[1] + later[1])


def pick_pair(flag, first, second):
    return (jnp.where(flag, first[0], second[0]), jnp.where(flag, first[1], second[1]))


def combine_levels(state, from_higher, bits):
    position = lax.axis_index("seq")
    prefix, total = state
    for bit in bits:
        other = partner(total, "seq", bit)
        high_half = position // (1 << bit) % 2 == 1
        takes_other = jnp.logical_not(high_half) if from_higher else high_half
        prefix = pick_pair(takes_other, join_pairs(other, prefix), prefix)
        total = pick_pair(takes_other, join_pairs(other, total), join_pairs(total, other))
    return prefix, total


def identity_pair(heads, shape):
    return (jnp.ones((heads,), jnp.float32), jnp.zeros((heads,) + shape, jnp.float32))


def chain_kernel(bits, shift, a_ref, es_ref, eg_ref, pa_ref, pes_ref, peg_ref, tot_a, tot_e, recv_a, recv_e, send_sem, recv_sem):
    e_refs, pe_refs = (es_ref, eg_ref), (pes_ref, peg_ref)
    seq_pos, dp_pos = lax.axis_index("seq"), lax.axis_index("dp")
    levels = len(bits)
    chains, groups = len(e_refs), es_ref.shape[0]
    highs, partners = [], []
    for bit in bits:
        mask = 1 << bit
        up = seq_pos // mask % 2
        highs.append(up == 1)
        partners.append((dp_pos, seq_pos + mask - 2 * mask * up))
    barrier = pltpu.get_barrier_semaphore()
    for device in partners:
        pl.semaphore_signal(barrier, inc=1, device_id=device, device_id_type=MESH)
    pl.semaphore_wait(barrier, levels)
    pa_ref[...] = jnp.ones(pa_ref.shape, jnp.float32)
    for pe_ref in pe_refs:
        pe_ref[...] = jnp.zeros(pe_ref.shape, jnp.float32)
    for slot in range(levels + shift * (groups - 1)):
        active = [(g, slot - shift * g) for g in range(groups) if 0 <= slot - shift * g < levels]
        work = []
        for g, lev in active:
            src_a = a_ref.at[g] if lev == 0 else tot_a.at[(lev - 1) % 2, g]
            src_e = [e_refs[c].at[g] if lev == 0 else tot_e.at[(lev - 1) % 2, c, g] for c in range(chains)]
            if lev == levels - 1:
                needed = highs[lev].astype(jnp.int32)
                source = tot_e.at[(lev - 1) % 2, needed, g]
                pairs = [(src_a, recv_a.at[lev, g]), (source, recv_e.at[lev, 0, g])]
            else:
                pairs = [(src_a, recv_a.at[lev, g])] + [(src_e[c], recv_e.at[lev, c, g]) for c in range(chains)]
            copies = []
            for k, (source, target) in enumerate(pairs):
                index = (lev * groups + g) * (chains + 1) + k
                copy = pltpu.make_async_remote_copy(
                    src_ref=source,
                    dst_ref=target,
                    send_sem=send_sem.at[index],
                    recv_sem=recv_sem.at[index],
                    device_id=partners[lev],
                    device_id_type=MESH,
                )
                copy.start()
                copies.append(copy)
            work.append((g, lev, src_a, src_e, copies))
        for g, lev, src_a, src_e, copies in work:
            for copy in copies:
                copy.wait()
            o_a = recv_a[lev, g]
            t_a = src_a[...]
            last = lev == levels - 1
            if not last:
                tot_a[lev % 2, g] = o_a * t_a
            for c in range(chains):
                takes = jnp.logical_not(highs[lev]) if c == 1 else highs[lev]
                o_e = recv_e[lev, 0 if last else c, g]
                p_a = pa_ref[c, g]
                p_e = pe_refs[c][g]
                pe_refs[c][g] = jnp.where(takes, p_a * o_e + p_e, p_e)
                pa_ref[c, g] = jnp.where(takes, o_a * p_a, p_a)
                if not last:
                    t_e = src_e[c][...]
                    tot_e[lev % 2, c, g] = jnp.where(takes, t_a * o_e + t_e, o_a * t_e + o_e)


def chip_scan(mines):
    heads = mines[0][0].shape[0]
    groups = 2
    quarter = heads // groups
    state, width = mines[0][1].shape[1:]
    rows = state * width // 128
    levels = lax.axis_size("seq").bit_length() - 1
    bits = tuple(range(1, levels))
    shift = (levels - 1) // 2
    a_in = jnp.broadcast_to(mines[0][0].reshape(groups, quarter, 1, 1), (groups, quarter, 1, 128))
    e_in = [mine[1].reshape(groups, quarter, rows, 128) for mine in mines]
    chains = len(mines)
    copies = len(bits) * groups * (chains + 1)
    vmem = pl.BlockSpec(memory_space=pltpu.VMEM)
    pa, pes, peg = pl.pallas_call(
        functools.partial(chain_kernel, bits, shift),
        out_shape=(
            jax.ShapeDtypeStruct((chains, groups, quarter, 1, 128), jnp.float32),
            jax.ShapeDtypeStruct((groups, quarter, rows, 128), jnp.float32),
            jax.ShapeDtypeStruct((groups, quarter, rows, 128), jnp.float32),
        ),
        in_specs=[vmem] * 3,
        out_specs=(vmem, vmem, vmem),
        scratch_shapes=[
            pltpu.VMEM((2, groups, quarter, 1, 128), jnp.float32),
            pltpu.VMEM((2, chains, groups, quarter, rows, 128), jnp.float32),
            pltpu.VMEM((len(bits), groups, quarter, 1, 128), jnp.float32),
            pltpu.VMEM((len(bits), chains, groups, quarter, rows, 128), jnp.float32),
            pltpu.SemaphoreType.DMA((copies,)),
            pltpu.SemaphoreType.DMA((copies,)),
        ],
        compiler_params=pltpu.CompilerParams(collective_id=1, has_side_effects=True),
    )(a_in, *e_in)
    return [(pa[c, :, :, 0, 0].reshape(heads), pe.reshape(heads, state, width)) for c, pe in enumerate((pes, peg))]


def combine_chains(owns):
    heads = owns[0][0].shape[0]
    half = heads // 2
    shape = owns[0][1].shape[1:]
    core = lax.axis_index("seq") % 2
    directions = (False, True)
    in_chips, mines = [], []
    for own, from_higher in zip(owns, directions):
        in_chip, chip_total = combine_levels((identity_pair(heads, shape), own), from_higher, [0])
        in_chips.append(in_chip)
        mines.append(tuple(lax.dynamic_slice_in_dim(part, core * half, half, 0) for part in chip_total))
    results = []
    for across, in_chip in zip(chip_scan(mines), in_chips):
        sibling = partner(across, "seq", 0)
        low = pick_pair(core == 0, across, sibling)
        high = pick_pair(core == 0, sibling, across)
        full = tuple(jnp.concatenate([a, b], axis=0) for a, b in zip(low, high))
        results.append(join_pairs(full, in_chip))
    return results


def flat_bit_order(seq_bits, bits, near):
    order = []
    for b in near + list(range(bits)):
        if b < bits and b not in order:
            order.append(b)
    return order


def halving_kernel(seq_bits, orders, scale, *refs):
    lanes = len(orders)
    steps = len(orders[0])
    bufs, final_ref, scratch = refs[:lanes], refs[lanes], refs[lanes + 1:]
    small = sum(1 for step in range(steps) if (2 ** (steps - 1 - step)) % 8)
    per_lane = steps + steps + small
    send_sem, recv_sem = scratch[lanes * per_lane], scratch[lanes * per_lane + 1]
    seq_pos, dp_pos = lax.axis_index("seq"), lax.axis_index("dp")
    targets = {}
    for bit in range(steps):
        if bit < seq_bits:
            mask = 1 << bit
            mine = seq_pos // mask % 2
            targets[bit] = (mine, (dp_pos, seq_pos + mask - 2 * mask * mine))
        else:
            mask = 1 << (bit - seq_bits)
            mine = dp_pos // mask % 2
            targets[bit] = (mine, (dp_pos + mask - 2 * mask * mine, seq_pos))
    barrier = pltpu.get_barrier_semaphore()
    for bit in range(steps):
        pl.semaphore_signal(barrier, inc=1, device_id=targets[bit][1], device_id_type=MESH)
    pl.semaphore_wait(barrier, steps)
    currents = list(bufs)
    for step in range(steps):
        pending = []
        for lane in range(lanes):
            base = scratch[lane * per_lane:(lane + 1) * per_lane]
            recvs, accs, stages = base[:steps], base[steps:2 * steps], base[2 * steps:]
            mine, device = targets[orders[lane][step]]
            current = currents[lane]
            half = recvs[step].shape[0]
            if half % 8 == 0:
                source = current.at[pl.ds(pl.multiple_of((1 - mine) * half, 8), half)]
            else:
                source = stages[step - (steps - small)]
                source[...] = jnp.where(mine == 1, current[0:half], current[half:2 * half])
            copy = pltpu.make_async_remote_copy(
                src_ref=source,
                dst_ref=recvs[step],
                send_sem=send_sem.at[lane * steps + step],
                recv_sem=recv_sem.at[lane * steps + step],
                device_id=device,
                device_id_type=MESH,
            )
            copy.start()
            pending.append((lane, copy, mine, half, current, recvs[step], accs[step]))
        for lane, copy, mine, half, current, received, acc in pending:
            if half % 8 == 0:
                keep = current[pl.ds(pl.multiple_of(mine * half, 8), half)]
            else:
                keep = jnp.where(mine == 1, current[half:2 * half], current[0:half])
            copy.wait()
            acc[...] = keep + received[...]
            currents[lane] = acc
    rows, width = final_ref.shape[0], final_ref.shape[1] // lanes
    for lane in range(lanes):
        for row in range(rows):
            final_ref[row:row + 1, lane * width:(lane + 1) * width] = currents[lane][0:1, row * width:(row + 1) * width] * scale


def scatter_sum(product, scale):
    dp_size, seq_size = lax.axis_size("dp"), lax.axis_size("seq")
    seq_bits = seq_size.bit_length() - 1
    bits = seq_bits + dp_size.bit_length() - 1
    rows, cols = product.shape
    block = rows // (dp_size * seq_size)
    s = seq_bits
    orders = [
        flat_bit_order(s, bits, [0, 1, 3, s + 1, 2, 4, s + 2, s, s + 3]),
        flat_bit_order(s, bits, [0, 3, s + 1, 1, 4, s + 2, 2, s, s + 3]),
    ]
    lanes = len(orders)
    width = cols // lanes
    bufs = []
    for lane, order in enumerate(orders):
        part = product[:, lane * width:(lane + 1) * width].reshape((2,) * bits + (block * width,))
        part = part.transpose([bits - 1 - b for b in order] + [bits]).reshape(2**bits, block * width)
        bufs.append(part)
    sizes = [2 ** (bits - 1 - step) for step in range(bits)]
    scratch = []
    for lane in range(lanes):
        scratch += [pltpu.VMEM((size, block * width), jnp.float32) for size in sizes]
        scratch += [pltpu.VMEM((size, block * width), jnp.float32) for size in sizes]
        scratch += [pltpu.VMEM((size, block * width), jnp.float32) for size in sizes if size % 8]
    scratch += [pltpu.SemaphoreType.DMA((lanes * bits,)), pltpu.SemaphoreType.DMA((lanes * bits,))]
    vmem = pl.BlockSpec(memory_space=pltpu.VMEM)
    return pl.pallas_call(
        functools.partial(halving_kernel, seq_bits, orders, scale),
        out_shape=jax.ShapeDtypeStruct((block, cols), jnp.float32),
        in_specs=[vmem] * lanes,
        out_specs=vmem,
        scratch_shapes=scratch,
        compiler_params=pltpu.CompilerParams(collective_id=0, has_side_effects=True),
    )(*bufs)


def local(normed, values, cotangent, w_bc, rate_index, starts):
    hidden = normed[0]
    length = hidden.shape[0]
    heads = rate_index.shape[1]
    width = values.shape[2]
    head_dim = width // heads
    state = w_bc.shape[1] // 2
    proj = jnp.dot(hidden, w_bc, preferred_element_type=jnp.float32).astype(jnp.bfloat16)
    bmat = proj[:, :state].astype(jnp.float32)
    cmat = proj[:, state:].astype(jnp.float32)
    levels_table = rate_logs()
    matches = rate_index[0][:, :, None] == jnp.arange(RATES)[None, None, :]
    logrates = jnp.sum(jnp.where(matches, levels_table[None, None, :], 0.0), axis=2)
    lower_mat, cumulative, end_weight = decay_parts(logrates, starts[0])
    vals = values[0].astype(jnp.float32).reshape(length, heads, head_dim)
    cots = cotangent[0].astype(jnp.float32).reshape(length, heads, head_dim)
    decay_total = cumulative[:, -1]
    ends = jnp.einsum("hk,kn,khp->hpn", end_weight, bmat, vals, precision=highest)
    feeds = jnp.einsum("hk,kn,khp->hpn", cumulative, cmat, cots, precision=highest)
    before_pair, after_pair = combine_chains([(decay_total, ends), (decay_total, feeds)])
    before, after = before_pair[1], after_pair[1]
    scores = jnp.dot(cmat, bmat.T, precision=highest)
    mixed = lower_mat * scores[None]
    grad_vals = jnp.einsum("hts,thp->shp", mixed, cots, precision=highest)
    grad_vals = grad_vals + end_weight.T[:, :, None] * jnp.einsum(
        "sn,hpn->shp", bmat, after, precision=highest
    )
    paired = lower_mat * jnp.einsum("thp,shp->hts", cots, vals, precision=highest)
    grad_b = jnp.einsum("hts,tn->sn", paired, cmat, precision=highest)
    grad_b = grad_b + jnp.einsum("hs,shp,hpn->sn", end_weight, vals, after, precision=highest)
    grad_c = jnp.einsum("hts,sn->tn", paired, bmat, precision=highest)
    grad_c = grad_c + jnp.einsum("ht,thp,hpn->tn", cumulative, cots, before, precision=highest)
    grad_values = grad_vals.reshape(length, width).astype(jnp.bfloat16)[None]
    grad_bc = jnp.concatenate([grad_b, grad_c], axis=1).astype(jnp.bfloat16)
    scale = 1.0 / (lax.axis_size("dp") * lax.axis_size("seq") * length)
    product = lax.dot_general(
        hidden, grad_bc, (((0,), (0,)), ((), ())), preferred_element_type=jnp.float32
    )
    grad_wbc = scatter_sum(product, scale)
    return (grad_values, grad_wbc)


def solution(mesh):
    placed = (
        P("dp", "seq", None),
        P("dp", "seq", None),
        P("dp", "seq", None),
        P(),
        P("dp", None, "seq"),
        P("dp", "seq"),
    )
    return jax.shard_map(
        local,
        mesh=mesh,
        in_specs=placed,
        out_specs=(P("dp", "seq", None), P(("dp", "seq"), None)),
        check_vma=False,
    )
```

```python
import functools

import jax
import jax.numpy as jnp
from jax import lax
from jax.experimental import pallas as pl
from jax.experimental.pallas import tpu as pltpu
from jax.sharding import PartitionSpec as P

MESH = pl.DeviceIdType.MESH

RATES = 16


highest = lax.Precision.HIGHEST


def partner(value, axis, apart):
    mask = 2**apart
    pairs = [(source, source ^ mask) for source in range(lax.axis_size(axis))]
    return lax.ppermute(value, axis, pairs)


def rate_logs():
    ranks = jnp.arange(RATES).astype(jnp.float32)
    return -0.0001 * jnp.power(jnp.float32(500.0), ranks / (RATES - 1))


def decay_parts(logrates, flags):
    length = flags.shape[0]
    sums = jnp.cumsum(logrates, axis=1)
    segment = jnp.cumsum(flags)
    order = jnp.arange(length)
    inside = (segment[:, None] == segment[None, :]) & (order[:, None] >= order[None, :])
    spread = sums[:, :, None] - sums[:, None, :]
    lower_mat = jnp.where(inside[None], jnp.exp(jnp.where(inside[None], spread, 0.0)), 0.0)
    cumulative = jnp.where((segment == 0)[None, :], jnp.exp(sums), 0.0)
    end_weight = lower_mat[:, length - 1, :]
    return (lower_mat, cumulative, end_weight)


def join_pairs(earlier, later):
    return (earlier[0] * later[0], later[0][:, None, None] * earlier[1] + later[1])


def pick_pair(flag, first, second):
    return (jnp.where(flag, first[0], second[0]), jnp.where(flag, first[1], second[1]))


def combine_levels(state, from_higher, bits):
    position = lax.axis_index("seq")
    prefix, total = state
    for bit in bits:
        other = partner(total, "seq", bit)
        high_half = position // (1 << bit) % 2 == 1
        takes_other = jnp.logical_not(high_half) if from_higher else high_half
        prefix = pick_pair(takes_other, join_pairs(other, prefix), prefix)
        total = pick_pair(takes_other, join_pairs(other, total), join_pairs(total, other))
    return prefix, total


def identity_pair(heads, shape):
    return (jnp.ones((heads,), jnp.float32), jnp.zeros((heads,) + shape, jnp.float32))


def chain_kernel(bits, shift, a_ref, es_ref, eg_ref, fa_ref, fes_ref, feg_ref, pa_ref, pes_ref, peg_ref, tot_a, tot_e, recv_a, recv_e, sib_a, sib_e, send_sem, recv_sem):
    e_refs, pe_refs, full_refs = (es_ref, eg_ref), (pes_ref, peg_ref), (fes_ref, feg_ref)
    seq_pos, dp_pos = lax.axis_index("seq"), lax.axis_index("dp")
    levels = len(bits)
    chains, groups = len(e_refs), es_ref.shape[0]
    highs, partners = [], []
    for bit in bits:
        mask = 1 << bit
        up = seq_pos // mask % 2
        highs.append(up == 1)
        partners.append((dp_pos, seq_pos + mask - 2 * mask * up))
    core = seq_pos % 2
    sibling = (dp_pos, seq_pos + 1 - 2 * core)
    barrier = pltpu.get_barrier_semaphore()
    for device in partners + [sibling]:
        pl.semaphore_signal(barrier, inc=1, device_id=device, device_id_type=MESH)
    pl.semaphore_wait(barrier, levels + 1)
    pa_ref[...] = jnp.ones(pa_ref.shape, jnp.float32)
    for pe_ref in pe_refs:
        pe_ref[...] = jnp.zeros(pe_ref.shape, jnp.float32)
    for slot in range(levels + shift * (groups - 1)):
        active = [(g, slot - shift * g) for g in range(groups) if 0 <= slot - shift * g < levels]
        work = []
        for g, lev in active:
            src_a = a_ref.at[g] if lev == 0 else tot_a.at[(lev - 1) % 2, g]
            src_e = [e_refs[c].at[g] if lev == 0 else tot_e.at[(lev - 1) % 2, c, g] for c in range(chains)]
            if lev == levels - 1:
                needed = highs[lev].astype(jnp.int32)
                source = tot_e.at[(lev - 1) % 2, needed, g]
                pairs = [(src_a, recv_a.at[lev, g]), (source, recv_e.at[lev, 0, g])]
            else:
                pairs = [(src_a, recv_a.at[lev, g])] + [(src_e[c], recv_e.at[lev, c, g]) for c in range(chains)]
            copies = []
            for k, (source, target) in enumerate(pairs):
                index = (lev * groups + g) * (chains + 1) + k
                copy = pltpu.make_async_remote_copy(
                    src_ref=source,
                    dst_ref=target,
                    send_sem=send_sem.at[index],
                    recv_sem=recv_sem.at[index],
                    device_id=partners[lev],
                    device_id_type=MESH,
                )
                copy.start()
                copies.append(copy)
            work.append((g, lev, src_a, src_e, copies))
        for g, lev, src_a, src_e, copies in work:
            for copy in copies:
                copy.wait()
            o_a = recv_a[lev, g]
            t_a = src_a[...]
            last = lev == levels - 1
            if not last:
                tot_a[lev % 2, g] = o_a * t_a
            for c in range(chains):
                takes = jnp.logical_not(highs[lev]) if c == 1 else highs[lev]
                o_e = recv_e[lev, 0 if last else c, g]
                p_a = pa_ref[c, g]
                p_e = pe_refs[c][g]
                pe_refs[c][g] = jnp.where(takes, p_a * o_e + p_e, p_e)
                pa_ref[c, g] = jnp.where(takes, o_a * p_a, p_a)
                if not last:
                    t_e = src_e[c][...]
                    tot_e[lev % 2, c, g] = jnp.where(takes, t_a * o_e + t_e, o_a * t_e + o_e)
    base = levels * groups * (chains + 1)
    finals = []
    for c in range(chains):
        for k, (source, target) in enumerate(((pa_ref.at[c], sib_a.at[c]), (pe_refs[c], sib_e.at[c]))):
            copy = pltpu.make_async_remote_copy(
                src_ref=source,
                dst_ref=target,
                send_sem=send_sem.at[base + 2 * c + k],
                recv_sem=recv_sem.at[base + 2 * c + k],
                device_id=sibling,
                device_id_type=MESH,
            )
            copy.start()
            finals.append(copy)
    for c in range(chains):
        fa_ref[c, core] = pa_ref[c]
        full_refs[c][core] = pe_refs[c][...]
    for copy in finals:
        copy.wait()
    for c in range(chains):
        fa_ref[c, 1 - core] = sib_a[c]
        full_refs[c][1 - core] = sib_e[c]


def chip_scan(mines):
    heads = mines[0][0].shape[0]
    groups = 2
    quarter = heads // groups
    state, width = mines[0][1].shape[1:]
    rows = state * width // 128
    levels = lax.axis_size("seq").bit_length() - 1
    bits = tuple(range(1, levels))
    shift = (levels - 1) // 2
    a_in = jnp.broadcast_to(mines[0][0].reshape(groups, quarter, 1, 1), (groups, quarter, 1, 128))
    e_in = [mine[1].reshape(groups, quarter, rows, 128) for mine in mines]
    chains = len(mines)
    copies = len(bits) * groups * (chains + 1) + 2 * chains
    vmem = pl.BlockSpec(memory_space=pltpu.VMEM)
    fa, fes, feg = pl.pallas_call(
        functools.partial(chain_kernel, bits, shift),
        out_shape=(
            jax.ShapeDtypeStruct((chains, 2, groups, quarter, 1, 128), jnp.float32),
            jax.ShapeDtypeStruct((2, groups, quarter, rows, 128), jnp.float32),
            jax.ShapeDtypeStruct((2, groups, quarter, rows, 128), jnp.float32),
        ),
        in_specs=[vmem] * 3,
        out_specs=(vmem, vmem, vmem),
        scratch_shapes=[
            pltpu.VMEM((chains, groups, quarter, 1, 128), jnp.float32),
            pltpu.VMEM((groups, quarter, rows, 128), jnp.float32),
            pltpu.VMEM((groups, quarter, rows, 128), jnp.float32),
            pltpu.VMEM((2, groups, quarter, 1, 128), jnp.float32),
            pltpu.VMEM((2, chains, groups, quarter, rows, 128), jnp.float32),
            pltpu.VMEM((len(bits), groups, quarter, 1, 128), jnp.float32),
            pltpu.VMEM((len(bits), chains, groups, quarter, rows, 128), jnp.float32),
            pltpu.VMEM((chains, groups, quarter, 1, 128), jnp.float32),
            pltpu.VMEM((chains, groups, quarter, rows, 128), jnp.float32),
            pltpu.SemaphoreType.DMA((copies,)),
            pltpu.SemaphoreType.DMA((copies,)),
        ],
        compiler_params=pltpu.CompilerParams(collective_id=1, has_side_effects=True),
    )(a_in, *e_in)
    return [
        (fa[c, :, :, :, 0, 0].reshape(2 * heads), fe.reshape(2 * heads, state, width))
        for c, fe in enumerate((fes, feg))
    ]


def combine_chains(owns):
    heads = owns[0][0].shape[0]
    half = heads // 2
    shape = owns[0][1].shape[1:]
    core = lax.axis_index("seq") % 2
    directions = (False, True)
    in_chips, mines = [], []
    for own, from_higher in zip(owns, directions):
        in_chip, chip_total = combine_levels((identity_pair(heads, shape), own), from_higher, [0])
        in_chips.append(in_chip)
        mines.append(tuple(lax.dynamic_slice_in_dim(part, core * half, half, 0) for part in chip_total))
    return [join_pairs(full, in_chip) for full, in_chip in zip(chip_scan(mines), in_chips)]


def flat_bit_order(seq_bits, bits, near):
    order = []
    for b in near + list(range(bits)):
        if b < bits and b not in order:
            order.append(b)
    return order


def halving_kernel(seq_bits, orders, scale, *refs):
    lanes = len(orders)
    steps = len(orders[0])
    bufs, final_ref, scratch = refs[:lanes], refs[lanes], refs[lanes + 1:]
    small = sum(1 for step in range(steps) if (2 ** (steps - 1 - step)) % 8)
    per_lane = steps + steps + small
    send_sem, recv_sem = scratch[lanes * per_lane], scratch[lanes * per_lane + 1]
    seq_pos, dp_pos = lax.axis_index("seq"), lax.axis_index("dp")
    targets = {}
    for bit in range(steps):
        if bit < seq_bits:
            mask = 1 << bit
            mine = seq_pos // mask % 2
            targets[bit] = (mine, (dp_pos, seq_pos + mask - 2 * mask * mine))
        else:
            mask = 1 << (bit - seq_bits)
            mine = dp_pos // mask % 2
            targets[bit] = (mine, (dp_pos + mask - 2 * mask * mine, seq_pos))
    barrier = pltpu.get_barrier_semaphore()
    for bit in range(steps):
        pl.semaphore_signal(barrier, inc=1, device_id=targets[bit][1], device_id_type=MESH)
    pl.semaphore_wait(barrier, steps)
    currents = list(bufs)
    for step in range(steps):
        pending = []
        for lane in range(lanes):
            base = scratch[lane * per_lane:(lane + 1) * per_lane]
            recvs, accs, stages = base[:steps], base[steps:2 * steps], base[2 * steps:]
            mine, device = targets[orders[lane][step]]
            current = currents[lane]
            half = recvs[step].shape[0]
            if half % 8 == 0:
                source = current.at[pl.ds(pl.multiple_of((1 - mine) * half, 8), half)]
            else:
                source = stages[step - (steps - small)]
                source[...] = jnp.where(mine == 1, current[0:half], current[half:2 * half])
            copy = pltpu.make_async_remote_copy(
                src_ref=source,
                dst_ref=recvs[step],
                send_sem=send_sem.at[lane * steps + step],
                recv_sem=recv_sem.at[lane * steps + step],
                device_id=device,
                device_id_type=MESH,
            )
            copy.start()
            pending.append((lane, copy, mine, half, current, recvs[step], accs[step]))
        for lane, copy, mine, half, current, received, acc in pending:
            if half % 8 == 0:
                keep = current[pl.ds(pl.multiple_of(mine * half, 8), half)]
            else:
                keep = jnp.where(mine == 1, current[half:2 * half], current[0:half])
            copy.wait()
            acc[...] = keep + received[...]
            currents[lane] = acc
    rows, width = final_ref.shape[0], final_ref.shape[1] // lanes
    for lane in range(lanes):
        for row in range(rows):
            final_ref[row:row + 1, lane * width:(lane + 1) * width] = currents[lane][0:1, row * width:(row + 1) * width] * scale


def scatter_sum(product, scale):
    dp_size, seq_size = lax.axis_size("dp"), lax.axis_size("seq")
    seq_bits = seq_size.bit_length() - 1
    bits = seq_bits + dp_size.bit_length() - 1
    rows, cols = product.shape
    block = rows // (dp_size * seq_size)
    s = seq_bits
    orders = [
        flat_bit_order(s, bits, [0, 1, 3, s + 1, 2, 4, s + 2, s, s + 3]),
        flat_bit_order(s, bits, [0, 3, s + 1, 1, 4, s + 2, 2, s, s + 3]),
    ]
    lanes = len(orders)
    width = cols // lanes
    bufs = []
    for lane, order in enumerate(orders):
        part = product[:, lane * width:(lane + 1) * width].reshape((2,) * bits + (block * width,))
        part = part.transpose([bits - 1 - b for b in order] + [bits]).reshape(2**bits, block * width)
        bufs.append(part)
    sizes = [2 ** (bits - 1 - step) for step in range(bits)]
    scratch = []
    for lane in range(lanes):
        scratch += [pltpu.VMEM((size, block * width), jnp.float32) for size in sizes]
        scratch += [pltpu.VMEM((size, block * width), jnp.float32) for size in sizes]
        scratch += [pltpu.VMEM((size, block * width), jnp.float32) for size in sizes if size % 8]
    scratch += [pltpu.SemaphoreType.DMA((lanes * bits,)), pltpu.SemaphoreType.DMA((lanes * bits,))]
    vmem = pl.BlockSpec(memory_space=pltpu.VMEM)
    return pl.pallas_call(
        functools.partial(halving_kernel, seq_bits, orders, scale),
        out_shape=jax.ShapeDtypeStruct((block, cols), jnp.float32),
        in_specs=[vmem] * lanes,
        out_specs=vmem,
        scratch_shapes=scratch,
        compiler_params=pltpu.CompilerParams(collective_id=0, has_side_effects=True),
    )(*bufs)


def local(normed, values, cotangent, w_bc, rate_index, starts):
    hidden = normed[0]
    length = hidden.shape[0]
    heads = rate_index.shape[1]
    width = values.shape[2]
    head_dim = width // heads
    state = w_bc.shape[1] // 2
    proj = jnp.dot(hidden, w_bc, preferred_element_type=jnp.float32).astype(jnp.bfloat16)
    bmat = proj[:, :state].astype(jnp.float32)
    cmat = proj[:, state:].astype(jnp.float32)
    levels_table = rate_logs()
    matches = rate_index[0][:, :, None] == jnp.arange(RATES)[None, None, :]
    logrates = jnp.sum(jnp.where(matches, levels_table[None, None, :], 0.0), axis=2)
    lower_mat, cumulative, end_weight = decay_parts(logrates, starts[0])
    vals = values[0].astype(jnp.float32).reshape(length, heads, head_dim)
    cots = cotangent[0].astype(jnp.float32).reshape(length, heads, head_dim)
    decay_total = cumulative[:, -1]
    ends = jnp.einsum("hk,kn,khp->hpn", end_weight, bmat, vals, precision=highest)
    feeds = jnp.einsum("hk,kn,khp->hpn", cumulative, cmat, cots, precision=highest)
    before_pair, after_pair = combine_chains([(decay_total, ends), (decay_total, feeds)])
    before, after = before_pair[1], after_pair[1]
    scores = jnp.dot(cmat, bmat.T, precision=highest)
    mixed = lower_mat * scores[None]
    grad_vals = jnp.einsum("hts,thp->shp", mixed, cots, precision=highest)
    grad_vals = grad_vals + end_weight.T[:, :, None] * jnp.einsum(
        "sn,hpn->shp", bmat, after, precision=highest
    )
    paired = lower_mat * jnp.einsum("thp,shp->hts", cots, vals, precision=highest)
    grad_b = jnp.einsum("hts,tn->sn", paired, cmat, precision=highest)
    grad_b = grad_b + jnp.einsum("hs,shp,hpn->sn", end_weight, vals, after, precision=highest)
    grad_c = jnp.einsum("hts,sn->tn", paired, bmat, precision=highest)
    grad_c = grad_c + jnp.einsum("ht,thp,hpn->tn", cumulative, cots, before, precision=highest)
    grad_values = grad_vals.reshape(length, width).astype(jnp.bfloat16)[None]
    grad_bc = jnp.concatenate([grad_b, grad_c], axis=1).astype(jnp.bfloat16)
    scale = 1.0 / (lax.axis_size("dp") * lax.axis_size("seq") * length)
    product = lax.dot_general(
        hidden, grad_bc, (((0,), (0,)), ((), ())), preferred_element_type=jnp.float32
    )
    grad_wbc = scatter_sum(product, scale)
    return (grad_values, grad_wbc)


def solution(mesh):
    placed = (
        P("dp", "seq", None),
        P("dp", "seq", None),
        P("dp", "seq", None),
        P(),
        P("dp", None, "seq"),
        P("dp", "seq"),
    )
    return jax.shard_map(
        local,
        mesh=mesh,
        in_specs=placed,
        out_specs=(P("dp", "seq", None), P(("dp", "seq"), None)),
        check_vma=False,
    )
```

```python
import functools

import jax
import jax.numpy as jnp
from jax import lax
from jax.experimental import pallas as pl
from jax.experimental.pallas import tpu as pltpu
from jax.sharding import PartitionSpec as P

MESH = pl.DeviceIdType.MESH

RATES = 16


highest = lax.Precision.HIGHEST


def partner(value, axis, apart):
    mask = 2**apart
    pairs = [(source, source ^ mask) for source in range(lax.axis_size(axis))]
    return lax.ppermute(value, axis, pairs)


def rate_logs():
    ranks = jnp.arange(RATES).astype(jnp.float32)
    return -0.0001 * jnp.power(jnp.float32(500.0), ranks / (RATES - 1))


def decay_parts(logrates, flags):
    length = flags.shape[0]
    sums = jnp.cumsum(logrates, axis=1)
    segment = jnp.cumsum(flags)
    order = jnp.arange(length)
    inside = (segment[:, None] == segment[None, :]) & (order[:, None] >= order[None, :])
    spread = sums[:, :, None] - sums[:, None, :]
    lower_mat = jnp.where(inside[None], jnp.exp(jnp.where(inside[None], spread, 0.0)), 0.0)
    cumulative = jnp.where((segment == 0)[None, :], jnp.exp(sums), 0.0)
    end_weight = lower_mat[:, length - 1, :]
    return (lower_mat, cumulative, end_weight)


def join_pairs(earlier, later):
    return (earlier[0] * later[0], later[0][:, None, None] * earlier[1] + later[1])


def pick_pair(flag, first, second):
    return (jnp.where(flag, first[0], second[0]), jnp.where(flag, first[1], second[1]))


def combine_levels(state, from_higher, bits):
    position = lax.axis_index("seq")
    prefix, total = state
    for bit in bits:
        other = partner(total, "seq", bit)
        high_half = position // (1 << bit) % 2 == 1
        takes_other = jnp.logical_not(high_half) if from_higher else high_half
        prefix = pick_pair(takes_other, join_pairs(other, prefix), prefix)
        total = pick_pair(takes_other, join_pairs(other, total), join_pairs(total, other))
    return prefix, total


def identity_pair(heads, shape):
    return (jnp.ones((heads,), jnp.float32), jnp.zeros((heads,) + shape, jnp.float32))


def chain_kernel(bits, shift, a_ref, es_ref, eg_ref, fes_ref, feg_ref, pa_ref, pes_ref, peg_ref, tot_a, tot_e, recv_a, recv_e, sib_e, start_a, start_e, zero_a, zero_e, send_sem, recv_sem):
    e_refs, pe_refs, full_refs = (es_ref, eg_ref), (pes_ref, peg_ref), (fes_ref, feg_ref)
    seq_pos, dp_pos = lax.axis_index("seq"), lax.axis_index("dp")
    levels = len(bits)
    chains, groups = len(e_refs), start_a.shape[0]
    highs, partners = [], []
    for bit in bits:
        mask = 1 << bit
        up = seq_pos // mask % 2
        highs.append(up == 1)
        partners.append((dp_pos, seq_pos + mask - 2 * mask * up))
    core = seq_pos % 2
    sibling = (dp_pos, seq_pos + 1 - 2 * core)
    barrier = pltpu.get_barrier_semaphore()
    for device in partners + [sibling]:
        pl.semaphore_signal(barrier, inc=1, device_id=device, device_id_type=MESH)
    pl.semaphore_wait(barrier, levels + 1)
    base = levels * groups * (chains + 1)
    first = [(a_ref, zero_a)] + [(e_refs[c], zero_e.at[c]) for c in range(chains)]
    opening = []
    for k, (source, target) in enumerate(first):
        copy = pltpu.make_async_remote_copy(
            src_ref=source,
            dst_ref=target,
            send_sem=send_sem.at[base + chains + k],
            recv_sem=recv_sem.at[base + chains + k],
            device_id=sibling,
            device_id_type=MESH,
        )
        copy.start()
        opening.append(copy)
    pa_ref[...] = jnp.ones(pa_ref.shape, jnp.float32)
    for pe_ref in pe_refs:
        pe_ref[...] = jnp.zeros(pe_ref.shape, jnp.float32)
    for copy in opening:
        copy.wait()
    on_top = core == 1
    takes_first = (on_top, jnp.logical_not(on_top))
    own_a, other_a = a_ref[core], zero_a[core]
    start_a[...] = own_a * other_a
    for c in range(chains):
        own_e, other_e = e_refs[c][core], zero_e[c, core]
        start_e[c] = jnp.where(takes_first[c], own_a * other_e + own_e, other_a * own_e + other_e)
    for slot in range(levels + shift * (groups - 1)):
        active = [(g, slot - shift * g) for g in range(groups) if 0 <= slot - shift * g < levels]
        work = []
        for g, lev in active:
            src_a = start_a.at[g] if lev == 0 else tot_a.at[(lev - 1) % 2, g]
            src_e = [start_e.at[c, g] if lev == 0 else tot_e.at[(lev - 1) % 2, c, g] for c in range(chains)]
            if lev == levels - 1:
                needed = highs[lev].astype(jnp.int32)
                source = tot_e.at[(lev - 1) % 2, needed, g]
                pairs = [(src_a, recv_a.at[lev, g]), (source, recv_e.at[lev, 0, g])]
            else:
                pairs = [(src_a, recv_a.at[lev, g])] + [(src_e[c], recv_e.at[lev, c, g]) for c in range(chains)]
            copies = []
            for k, (source, target) in enumerate(pairs):
                index = (lev * groups + g) * (chains + 1) + k
                copy = pltpu.make_async_remote_copy(
                    src_ref=source,
                    dst_ref=target,
                    send_sem=send_sem.at[index],
                    recv_sem=recv_sem.at[index],
                    device_id=partners[lev],
                    device_id_type=MESH,
                )
                copy.start()
                copies.append(copy)
            work.append((g, lev, src_a, src_e, copies))
        for g, lev, src_a, src_e, copies in work:
            for copy in copies:
                copy.wait()
            o_a = recv_a[lev, g]
            t_a = src_a[...]
            last = lev == levels - 1
            if not last:
                tot_a[lev % 2, g] = o_a * t_a
            for c in range(chains):
                takes = jnp.logical_not(highs[lev]) if c == 1 else highs[lev]
                o_e = recv_e[lev, 0 if last else c, g]
                p_a = pa_ref[c, g]
                p_e = pe_refs[c][g]
                pe_refs[c][g] = jnp.where(takes, p_a * o_e + p_e, p_e)
                pa_ref[c, g] = jnp.where(takes, o_a * p_a, p_a)
                if not last:
                    t_e = src_e[c][...]
                    tot_e[lev % 2, c, g] = jnp.where(takes, t_a * o_e + t_e, o_a * t_e + o_e)
    finals = []
    for c in range(chains):
        copy = pltpu.make_async_remote_copy(
            src_ref=pe_refs[c],
            dst_ref=sib_e.at[c],
            send_sem=send_sem.at[base + c],
            recv_sem=recv_sem.at[base + c],
            device_id=sibling,
            device_id_type=MESH,
        )
        copy.start()
        finals.append(copy)
    for c in range(chains):
        full_refs[c][core] = pe_refs[c][...]
    for copy in finals:
        copy.wait()
    for c in range(chains):
        full_refs[c][1 - core] = sib_e[c]
        whole = full_refs[c][...]
        full_refs[c][...] = jnp.where(takes_first[c], zero_a[...] * whole + zero_e[c], whole)


def combine_chains(decay_total, owns):
    heads, state, width = owns[0].shape
    halves, groups = 2, 2
    quarter = heads // (halves * groups)
    rows = state * width // 128
    levels = lax.axis_size("seq").bit_length() - 1
    bits = tuple(range(1, levels))
    shift = (levels - 1) // 2
    a_in = jnp.broadcast_to(decay_total.reshape(halves, groups, quarter, 1, 1), (halves, groups, quarter, 1, 128))
    e_in = [own.reshape(halves, groups, quarter, rows, 128) for own in owns]
    chains = len(owns)
    copies = len(bits) * groups * (chains + 1) + 2 * chains + 1
    vmem = pl.BlockSpec(memory_space=pltpu.VMEM)
    full = pl.pallas_call(
        functools.partial(chain_kernel, bits, shift),
        out_shape=tuple(jax.ShapeDtypeStruct((halves, groups, quarter, rows, 128), jnp.float32) for _ in owns),
        in_specs=[vmem] * 3,
        out_specs=(vmem, vmem),
        scratch_shapes=[
            pltpu.VMEM((chains, groups, quarter, 1, 128), jnp.float32),
            pltpu.VMEM((groups, quarter, rows, 128), jnp.float32),
            pltpu.VMEM((groups, quarter, rows, 128), jnp.float32),
            pltpu.VMEM((2, groups, quarter, 1, 128), jnp.float32),
            pltpu.VMEM((2, chains, groups, quarter, rows, 128), jnp.float32),
            pltpu.VMEM((len(bits), groups, quarter, 1, 128), jnp.float32),
            pltpu.VMEM((len(bits), chains, groups, quarter, rows, 128), jnp.float32),
            pltpu.VMEM((chains, groups, quarter, rows, 128), jnp.float32),
            pltpu.VMEM((groups, quarter, 1, 128), jnp.float32),
            pltpu.VMEM((chains, groups, quarter, rows, 128), jnp.float32),
            pltpu.VMEM((halves, groups, quarter, 1, 128), jnp.float32),
            pltpu.VMEM((chains, halves, groups, quarter, rows, 128), jnp.float32),
            pltpu.SemaphoreType.DMA((copies,)),
            pltpu.SemaphoreType.DMA((copies,)),
        ],
        compiler_params=pltpu.CompilerParams(collective_id=1, has_side_effects=True),
    )(a_in, *e_in)
    return [part.reshape(heads, state, width) for part in full]


def flat_bit_order(seq_bits, bits, near):
    order = []
    for b in near + list(range(bits)):
        if b < bits and b not in order:
            order.append(b)
    return order


def halving_kernel(seq_bits, orders, scale, *refs):
    lanes = len(orders)
    steps = len(orders[0])
    bufs, final_ref, scratch = refs[:lanes], refs[lanes], refs[lanes + 1:]
    small = sum(1 for step in range(steps) if (2 ** (steps - 1 - step)) % 8)
    per_lane = steps + steps + small
    send_sem, recv_sem = scratch[lanes * per_lane], scratch[lanes * per_lane + 1]
    seq_pos, dp_pos = lax.axis_index("seq"), lax.axis_index("dp")
    targets = {}
    for bit in range(steps):
        if bit < seq_bits:
            mask = 1 << bit
            mine = seq_pos // mask % 2
            targets[bit] = (mine, (dp_pos, seq_pos + mask - 2 * mask * mine))
        else:
            mask = 1 << (bit - seq_bits)
            mine = dp_pos // mask % 2
            targets[bit] = (mine, (dp_pos + mask - 2 * mask * mine, seq_pos))
    barrier = pltpu.get_barrier_semaphore()
    for bit in range(steps):
        pl.semaphore_signal(barrier, inc=1, device_id=targets[bit][1], device_id_type=MESH)
    pl.semaphore_wait(barrier, steps)
    currents = list(bufs)
    for step in range(steps):
        pending = []
        for lane in range(lanes):
            base = scratch[lane * per_lane:(lane + 1) * per_lane]
            recvs, accs, stages = base[:steps], base[steps:2 * steps], base[2 * steps:]
            mine, device = targets[orders[lane][step]]
            current = currents[lane]
            half = recvs[step].shape[0]
            if half % 8 == 0:
                source = current.at[pl.ds(pl.multiple_of((1 - mine) * half, 8), half)]
            else:
                source = stages[step - (steps - small)]
                source[...] = jnp.where(mine == 1, current[0:half], current[half:2 * half])
            copy = pltpu.make_async_remote_copy(
                src_ref=source,
                dst_ref=recvs[step],
                send_sem=send_sem.at[lane * steps + step],
                recv_sem=recv_sem.at[lane * steps + step],
                device_id=device,
                device_id_type=MESH,
            )
            copy.start()
            pending.append((lane, copy, mine, half, current, recvs[step], accs[step]))
        for lane, copy, mine, half, current, received, acc in pending:
            if half % 8 == 0:
                keep = current[pl.ds(pl.multiple_of(mine * half, 8), half)]
            else:
                keep = jnp.where(mine == 1, current[half:2 * half], current[0:half])
            copy.wait()
            acc[...] = keep + received[...]
            currents[lane] = acc
    rows, width = final_ref.shape[0], final_ref.shape[1] // lanes
    for lane in range(lanes):
        for row in range(rows):
            final_ref[row:row + 1, lane * width:(lane + 1) * width] = currents[lane][0:1, row * width:(row + 1) * width] * scale


def scatter_sum(product, scale):
    dp_size, seq_size = lax.axis_size("dp"), lax.axis_size("seq")
    seq_bits = seq_size.bit_length() - 1
    bits = seq_bits + dp_size.bit_length() - 1
    rows, cols = product.shape
    block = rows // (dp_size * seq_size)
    s = seq_bits
    orders = [
        flat_bit_order(s, bits, [0, 1, 3, s + 1, 2, 4, s + 2, s, s + 3]),
        flat_bit_order(s, bits, [0, 3, s + 1, 1, 4, s + 2, 2, s, s + 3]),
    ]
    lanes = len(orders)
    width = cols // lanes
    bufs = []
    for lane, order in enumerate(orders):
        part = product[:, lane * width:(lane + 1) * width].reshape((2,) * bits + (block * width,))
        part = part.transpose([bits - 1 - b for b in order] + [bits]).reshape(2**bits, block * width)
        bufs.append(part)
    sizes = [2 ** (bits - 1 - step) for step in range(bits)]
    scratch = []
    for lane in range(lanes):
        scratch += [pltpu.VMEM((size, block * width), jnp.float32) for size in sizes]
        scratch += [pltpu.VMEM((size, block * width), jnp.float32) for size in sizes]
        scratch += [pltpu.VMEM((size, block * width), jnp.float32) for size in sizes if size % 8]
    scratch += [pltpu.SemaphoreType.DMA((lanes * bits,)), pltpu.SemaphoreType.DMA((lanes * bits,))]
    vmem = pl.BlockSpec(memory_space=pltpu.VMEM)
    return pl.pallas_call(
        functools.partial(halving_kernel, seq_bits, orders, scale),
        out_shape=jax.ShapeDtypeStruct((block, cols), jnp.float32),
        in_specs=[vmem] * lanes,
        out_specs=vmem,
        scratch_shapes=scratch,
        compiler_params=pltpu.CompilerParams(collective_id=0, has_side_effects=True),
    )(*bufs)


def local(normed, values, cotangent, w_bc, rate_index, starts):
    hidden = normed[0]
    length = hidden.shape[0]
    heads = rate_index.shape[1]
    width = values.shape[2]
    head_dim = width // heads
    state = w_bc.shape[1] // 2
    proj = jnp.dot(hidden, w_bc, preferred_element_type=jnp.float32).astype(jnp.bfloat16)
    bmat = proj[:, :state].astype(jnp.float32)
    cmat = proj[:, state:].astype(jnp.float32)
    levels_table = rate_logs()
    matches = rate_index[0][:, :, None] == jnp.arange(RATES)[None, None, :]
    logrates = jnp.sum(jnp.where(matches, levels_table[None, None, :], 0.0), axis=2)
    lower_mat, cumulative, end_weight = decay_parts(logrates, starts[0])
    vals = values[0].astype(jnp.float32).reshape(length, heads, head_dim)
    cots = cotangent[0].astype(jnp.float32).reshape(length, heads, head_dim)
    decay_total = cumulative[:, -1]
    ends = jnp.einsum("hk,kn,khp->hpn", end_weight, bmat, vals, precision=highest)
    feeds = jnp.einsum("hk,kn,khp->hpn", cumulative, cmat, cots, precision=highest)
    before, after = combine_chains(decay_total, [ends, feeds])
    scores = jnp.dot(cmat, bmat.T, precision=highest)
    mixed = lower_mat * scores[None]
    grad_vals = jnp.einsum("hts,thp->shp", mixed, cots, precision=highest)
    grad_vals = grad_vals + end_weight.T[:, :, None] * jnp.einsum(
        "sn,hpn->shp", bmat, after, precision=highest
    )
    paired = lower_mat * jnp.einsum("thp,shp->hts", cots, vals, precision=highest)
    grad_b = jnp.einsum("hts,tn->sn", paired, cmat, precision=highest)
    grad_b = grad_b + jnp.einsum("hs,shp,hpn->sn", end_weight, vals, after, precision=highest)
    grad_c = jnp.einsum("hts,sn->tn", paired, bmat, precision=highest)
    grad_c = grad_c + jnp.einsum("ht,thp,hpn->tn", cumulative, cots, before, precision=highest)
    grad_values = grad_vals.reshape(length, width).astype(jnp.bfloat16)[None]
    grad_bc = jnp.concatenate([grad_b, grad_c], axis=1).astype(jnp.bfloat16)
    scale = 1.0 / (lax.axis_size("dp") * lax.axis_size("seq") * length)
    product = lax.dot_general(
        hidden, grad_bc, (((0,), (0,)), ((), ())), preferred_element_type=jnp.float32
    )
    grad_wbc = scatter_sum(product, scale)
    return (grad_values, grad_wbc)


def solution(mesh):
    placed = (
        P("dp", "seq", None),
        P("dp", "seq", None),
        P("dp", "seq", None),
        P(),
        P("dp", None, "seq"),
        P("dp", "seq"),
    )
    return jax.shard_map(
        local,
        mesh=mesh,
        in_specs=placed,
        out_specs=(P("dp", "seq", None), P(("dp", "seq"), None)),
        check_vma=False,
    )
```

```python
import functools

import jax
import jax.numpy as jnp
from jax import lax
from jax.experimental import pallas as pl
from jax.experimental.pallas import tpu as pltpu
from jax.sharding import PartitionSpec as P

MESH = pl.DeviceIdType.MESH

RATES = 16


highest = lax.Precision.HIGHEST


def partner(value, axis, apart):
    mask = 2**apart
    pairs = [(source, source ^ mask) for source in range(lax.axis_size(axis))]
    return lax.ppermute(value, axis, pairs)


def rate_logs():
    ranks = jnp.arange(RATES).astype(jnp.float32)
    return -0.0001 * jnp.power(jnp.float32(500.0), ranks / (RATES - 1))


def decay_parts(logrates, flags):
    length = flags.shape[0]
    sums = jnp.cumsum(logrates, axis=1)
    segment = jnp.cumsum(flags)
    order = jnp.arange(length)
    inside = (segment[:, None] == segment[None, :]) & (order[:, None] >= order[None, :])
    spread = sums[:, :, None] - sums[:, None, :]
    lower_mat = jnp.where(inside[None], jnp.exp(jnp.where(inside[None], spread, 0.0)), 0.0)
    cumulative = jnp.where((segment == 0)[None, :], jnp.exp(sums), 0.0)
    end_weight = lower_mat[:, length - 1, :]
    return (lower_mat, cumulative, end_weight)


def join_pairs(earlier, later):
    return (earlier[0] * later[0], later[0][:, None, None] * earlier[1] + later[1])


def pick_pair(flag, first, second):
    return (jnp.where(flag, first[0], second[0]), jnp.where(flag, first[1], second[1]))


def combine_levels(state, from_higher, bits):
    position = lax.axis_index("seq")
    prefix, total = state
    for bit in bits:
        other = partner(total, "seq", bit)
        high_half = position // (1 << bit) % 2 == 1
        takes_other = jnp.logical_not(high_half) if from_higher else high_half
        prefix = pick_pair(takes_other, join_pairs(other, prefix), prefix)
        total = pick_pair(takes_other, join_pairs(other, total), join_pairs(total, other))
    return prefix, total


def identity_pair(heads, shape):
    return (jnp.ones((heads,), jnp.float32), jnp.zeros((heads,) + shape, jnp.float32))


def chain_kernel(bits, shift, a_ref, es_ref, eg_ref, fes_ref, feg_ref, pa_ref, pes_ref, peg_ref, tot_a, tot_e, recv_a, recv_e, sib_e, start_a, start_e, zero_a, zero_e, send_sem, recv_sem):
    e_refs, pe_refs, full_refs = (es_ref, eg_ref), (pes_ref, peg_ref), (fes_ref, feg_ref)
    seq_pos, dp_pos = lax.axis_index("seq"), lax.axis_index("dp")
    levels = len(bits)
    chains, groups = len(e_refs), start_a.shape[0]
    highs, partners = [], []
    for bit in bits:
        mask = 1 << bit
        up = seq_pos // mask % 2
        highs.append(up == 1)
        partners.append((dp_pos, seq_pos + mask - 2 * mask * up))
    core = seq_pos % 2
    sibling = (dp_pos, seq_pos + 1 - 2 * core)
    barrier = pltpu.get_barrier_semaphore()
    for device in partners + [sibling]:
        pl.semaphore_signal(barrier, inc=1, device_id=device, device_id_type=MESH)
    pl.semaphore_wait(barrier, levels + 1)
    base = levels * groups * (chains + 1)
    first = [(a_ref, zero_a)] + [(e_refs[c], zero_e.at[c]) for c in range(chains)]
    opening = []
    for k, (source, target) in enumerate(first):
        copy = pltpu.make_async_remote_copy(
            src_ref=source,
            dst_ref=target,
            send_sem=send_sem.at[base + chains + k],
            recv_sem=recv_sem.at[base + chains + k],
            device_id=sibling,
            device_id_type=MESH,
        )
        copy.start()
        opening.append(copy)
    pa_ref[...] = jnp.ones(pa_ref.shape, jnp.float32)
    for pe_ref in pe_refs:
        pe_ref[...] = jnp.zeros(pe_ref.shape, jnp.float32)
    for copy in opening:
        copy.wait()
    on_top = core == 1
    takes_first = (on_top, jnp.logical_not(on_top))
    own_a, other_a = a_ref[core], zero_a[core]
    start_a[...] = own_a * other_a
    for c in range(chains):
        own_e, other_e = e_refs[c][core], zero_e[c, core]
        start_e[c] = jnp.where(takes_first[c], own_a * other_e + own_e, other_a * own_e + other_e)
    for slot in range(levels + shift * (groups - 1)):
        active = [(g, slot - shift * g) for g in range(groups) if 0 <= slot - shift * g < levels]
        work = []
        for g, lev in active:
            src_a = start_a.at[g] if lev == 0 else tot_a.at[(lev - 1) % 2, g]
            src_e = [start_e.at[c, g] if lev == 0 else tot_e.at[(lev - 1) % 2, c, g] for c in range(chains)]
            if lev == levels - 1:
                needed = highs[lev].astype(jnp.int32)
                source = tot_e.at[(lev - 1) % 2, needed, g]
                pairs = [(src_a, recv_a.at[lev, g]), (source, recv_e.at[lev, 0, g])]
            else:
                pairs = [(src_a, recv_a.at[lev, g])] + [(src_e[c], recv_e.at[lev, c, g]) for c in range(chains)]
            copies = []
            for k, (source, target) in enumerate(pairs):
                index = (lev * groups + g) * (chains + 1) + k
                copy = pltpu.make_async_remote_copy(
                    src_ref=source,
                    dst_ref=target,
                    send_sem=send_sem.at[index],
                    recv_sem=recv_sem.at[index],
                    device_id=partners[lev],
                    device_id_type=MESH,
                )
                copy.start()
                copies.append(copy)
            work.append((g, lev, src_a, src_e, copies))
        for g, lev, src_a, src_e, copies in work:
            for copy in copies:
                copy.wait()
            o_a = recv_a[lev, g]
            t_a = src_a[...]
            last = lev == levels - 1
            if not last:
                tot_a[lev % 2, g] = o_a * t_a
            for c in range(chains):
                takes = jnp.logical_not(highs[lev]) if c == 1 else highs[lev]
                o_e = recv_e[lev, 0 if last else c, g]
                p_a = pa_ref[c, g]
                p_e = pe_refs[c][g]
                pe_refs[c][g] = jnp.where(takes, p_a * o_e + p_e, p_e)
                pa_ref[c, g] = jnp.where(takes, o_a * p_a, p_a)
                if not last:
                    t_e = src_e[c][...]
                    tot_e[lev % 2, c, g] = jnp.where(takes, t_a * o_e + t_e, o_a * t_e + o_e)
    finals = []
    for c in range(chains):
        copy = pltpu.make_async_remote_copy(
            src_ref=pe_refs[c],
            dst_ref=sib_e.at[c],
            send_sem=send_sem.at[base + c],
            recv_sem=recv_sem.at[base + c],
            device_id=sibling,
            device_id_type=MESH,
        )
        copy.start()
        finals.append(copy)
    for c in range(chains):
        full_refs[c][core] = pe_refs[c][...]
    for copy in finals:
        copy.wait()
    for c in range(chains):
        full_refs[c][1 - core] = sib_e[c]
        whole = full_refs[c][...]
        full_refs[c][...] = jnp.where(takes_first[c], zero_a[...] * whole + zero_e[c], whole)


def combine_chains(decay_total, owns):
    heads, state, width = owns[0].shape
    halves, groups = 2, 2
    quarter = heads // (halves * groups)
    rows = state * width // 128
    levels = lax.axis_size("seq").bit_length() - 1
    bits = tuple(range(1, levels))
    shift = (levels - 1) // 2
    a_in = jnp.broadcast_to(decay_total.reshape(halves, groups, quarter, 1, 1), (halves, groups, quarter, 1, 128))
    e_in = [own.reshape(halves, groups, quarter, rows, 128) for own in owns]
    chains = len(owns)
    copies = len(bits) * groups * (chains + 1) + 2 * chains + 1
    vmem = pl.BlockSpec(memory_space=pltpu.VMEM)
    full = pl.pallas_call(
        functools.partial(chain_kernel, bits, shift),
        out_shape=tuple(jax.ShapeDtypeStruct((halves, groups, quarter, rows, 128), jnp.float32) for _ in owns),
        in_specs=[vmem] * 3,
        out_specs=(vmem, vmem),
        scratch_shapes=[
            pltpu.VMEM((chains, groups, quarter, 1, 128), jnp.float32),
            pltpu.VMEM((groups, quarter, rows, 128), jnp.float32),
            pltpu.VMEM((groups, quarter, rows, 128), jnp.float32),
            pltpu.VMEM((2, groups, quarter, 1, 128), jnp.float32),
            pltpu.VMEM((2, chains, groups, quarter, rows, 128), jnp.float32),
            pltpu.VMEM((len(bits), groups, quarter, 1, 128), jnp.float32),
            pltpu.VMEM((len(bits), chains, groups, quarter, rows, 128), jnp.float32),
            pltpu.VMEM((chains, groups, quarter, rows, 128), jnp.float32),
            pltpu.VMEM((groups, quarter, 1, 128), jnp.float32),
            pltpu.VMEM((chains, groups, quarter, rows, 128), jnp.float32),
            pltpu.VMEM((halves, groups, quarter, 1, 128), jnp.float32),
            pltpu.VMEM((chains, halves, groups, quarter, rows, 128), jnp.float32),
            pltpu.SemaphoreType.DMA((copies,)),
            pltpu.SemaphoreType.DMA((copies,)),
        ],
        compiler_params=pltpu.CompilerParams(collective_id=1, has_side_effects=True),
    )(a_in, *e_in)
    return [part.reshape(heads, state, width) for part in full]


def flat_bit_order(seq_bits, bits, near):
    order = []
    for b in near + list(range(bits)):
        if b < bits and b not in order:
            order.append(b)
    return order


def halving_kernel(seq_bits, orders, scale, *refs):
    lanes = len(orders)
    steps = len(orders[0])
    bufs, final_ref, scratch = refs[:lanes], refs[lanes], refs[lanes + 1:]
    small = sum(1 for step in range(steps) if (2 ** (steps - 1 - step)) % 8)
    per_lane = steps + steps + small
    send_sem, recv_sem = scratch[lanes * per_lane], scratch[lanes * per_lane + 1]
    seq_pos, dp_pos = lax.axis_index("seq"), lax.axis_index("dp")
    targets = {}
    for bit in range(steps):
        if bit < seq_bits:
            mask = 1 << bit
            mine = seq_pos // mask % 2
            targets[bit] = (mine, (dp_pos, seq_pos + mask - 2 * mask * mine))
        else:
            mask = 1 << (bit - seq_bits)
            mine = dp_pos // mask % 2
            targets[bit] = (mine, (dp_pos + mask - 2 * mask * mine, seq_pos))
    barrier = pltpu.get_barrier_semaphore()
    for bit in range(steps):
        pl.semaphore_signal(barrier, inc=1, device_id=targets[bit][1], device_id_type=MESH)
    pl.semaphore_wait(barrier, steps)
    currents = list(bufs)
    for step in range(steps):
        pending = []
        for lane in range(lanes):
            base = scratch[lane * per_lane:(lane + 1) * per_lane]
            recvs, accs, stages = base[:steps], base[steps:2 * steps], base[2 * steps:]
            mine, device = targets[orders[lane][step]]
            current = currents[lane]
            half = recvs[step].shape[0]
            if half % 8 == 0:
                source = current.at[pl.ds(pl.multiple_of((1 - mine) * half, 8), half)]
            else:
                source = stages[step - (steps - small)]
                source[...] = jnp.where(mine == 1, current[0:half], current[half:2 * half])
            copy = pltpu.make_async_remote_copy(
                src_ref=source,
                dst_ref=recvs[step],
                send_sem=send_sem.at[lane * steps + step],
                recv_sem=recv_sem.at[lane * steps + step],
                device_id=device,
                device_id_type=MESH,
            )
            copy.start()
            pending.append((lane, copy, mine, half, current, recvs[step], accs[step]))
        for lane, copy, mine, half, current, received, acc in pending:
            if half % 8 == 0:
                keep = current[pl.ds(pl.multiple_of(mine * half, 8), half)]
            else:
                keep = jnp.where(mine == 1, current[half:2 * half], current[0:half])
            copy.wait()
            acc[...] = keep + received[...]
            currents[lane] = acc
    rows, width = final_ref.shape[0], final_ref.shape[1] // lanes
    for lane in range(lanes):
        for row in range(rows):
            final_ref[row:row + 1, lane * width:(lane + 1) * width] = currents[lane][0:1, row * width:(row + 1) * width] * scale


def scatter_sum(product, scale):
    dp_size, seq_size = lax.axis_size("dp"), lax.axis_size("seq")
    seq_bits = seq_size.bit_length() - 1
    bits = seq_bits + dp_size.bit_length() - 1
    rows, cols = product.shape
    block = rows // (dp_size * seq_size)
    s = seq_bits
    orders = [
        flat_bit_order(s, bits, [0, 1, 3, s + 1, 2, 4, s + 2, s, s + 3]),
        flat_bit_order(s, bits, [0, 3, s + 1, 1, 4, s + 2, 2, s, s + 3]),
    ]
    lanes = len(orders)
    width = cols // lanes
    bufs = []
    for lane, order in enumerate(orders):
        part = product[:, lane * width:(lane + 1) * width].reshape(2**bits, block * width)
        source = [sum(((p >> (bits - 1 - i)) & 1) << b for i, b in enumerate(order)) for p in range(2**bits)]
        part = jnp.take(part, jnp.asarray(source, jnp.int32), axis=0)
        bufs.append(part)
    sizes = [2 ** (bits - 1 - step) for step in range(bits)]
    scratch = []
    for lane in range(lanes):
        scratch += [pltpu.VMEM((size, block * width), jnp.float32) for size in sizes]
        scratch += [pltpu.VMEM((size, block * width), jnp.float32) for size in sizes]
        scratch += [pltpu.VMEM((size, block * width), jnp.float32) for size in sizes if size % 8]
    scratch += [pltpu.SemaphoreType.DMA((lanes * bits,)), pltpu.SemaphoreType.DMA((lanes * bits,))]
    vmem = pl.BlockSpec(memory_space=pltpu.VMEM)
    return pl.pallas_call(
        functools.partial(halving_kernel, seq_bits, orders, scale),
        out_shape=jax.ShapeDtypeStruct((block, cols), jnp.float32),
        in_specs=[vmem] * lanes,
        out_specs=vmem,
        scratch_shapes=scratch,
        compiler_params=pltpu.CompilerParams(collective_id=0, has_side_effects=True),
    )(*bufs)


def local(normed, values, cotangent, w_bc, rate_index, starts):
    hidden = normed[0]
    length = hidden.shape[0]
    heads = rate_index.shape[1]
    width = values.shape[2]
    head_dim = width // heads
    state = w_bc.shape[1] // 2
    proj = jnp.dot(hidden, w_bc, preferred_element_type=jnp.float32).astype(jnp.bfloat16)
    bmat = proj[:, :state].astype(jnp.float32)
    cmat = proj[:, state:].astype(jnp.float32)
    levels_table = rate_logs()
    matches = rate_index[0][:, :, None] == jnp.arange(RATES)[None, None, :]
    logrates = jnp.sum(jnp.where(matches, levels_table[None, None, :], 0.0), axis=2)
    lower_mat, cumulative, end_weight = decay_parts(logrates, starts[0])
    vals = values[0].astype(jnp.float32).reshape(length, heads, head_dim)
    cots = cotangent[0].astype(jnp.float32).reshape(length, heads, head_dim)
    decay_total = cumulative[:, -1]
    ends = jnp.einsum("hk,kn,khp->hpn", end_weight, bmat, vals, precision=highest)
    feeds = jnp.einsum("hk,kn,khp->hpn", cumulative, cmat, cots, precision=highest)
    before, after = combine_chains(decay_total, [ends, feeds])
    scores = jnp.dot(cmat, bmat.T, precision=highest)
    mixed = lower_mat * scores[None]
    grad_vals = jnp.einsum("hts,thp->shp", mixed, cots, precision=highest)
    grad_vals = grad_vals + end_weight.T[:, :, None] * jnp.einsum(
        "sn,hpn->shp", bmat, after, precision=highest
    )
    paired = lower_mat * jnp.einsum("thp,shp->hts", cots, vals, precision=highest)
    grad_b = jnp.einsum("hts,tn->sn", paired, cmat, precision=highest)
    grad_b = grad_b + jnp.einsum("hs,shp,hpn->sn", end_weight, vals, after, precision=highest)
    grad_c = jnp.einsum("hts,sn->tn", paired, bmat, precision=highest)
    grad_c = grad_c + jnp.einsum("ht,thp,hpn->tn", cumulative, cots, before, precision=highest)
    grad_values = grad_vals.reshape(length, width).astype(jnp.bfloat16)[None]
    grad_bc = jnp.concatenate([grad_b, grad_c], axis=1).astype(jnp.bfloat16)
    scale = 1.0 / (lax.axis_size("dp") * lax.axis_size("seq") * length)
    product = lax.dot_general(
        hidden, grad_bc, (((0,), (0,)), ((), ())), preferred_element_type=jnp.float32
    )
    grad_wbc = scatter_sum(product, scale)
    return (grad_values, grad_wbc)


def solution(mesh):
    placed = (
        P("dp", "seq", None),
        P("dp", "seq", None),
        P("dp", "seq", None),
        P(),
        P("dp", None, "seq"),
        P("dp", "seq"),
    )
    return jax.shard_map(
        local,
        mesh=mesh,
        in_specs=placed,
        out_specs=(P("dp", "seq", None), P(("dp", "seq"), None)),
        check_vma=False,
    )
```

```python
import functools

import jax
import jax.numpy as jnp
from jax import lax
from jax.experimental import pallas as pl
from jax.experimental.pallas import tpu as pltpu
from jax.sharding import PartitionSpec as P

MESH = pl.DeviceIdType.MESH

RATES = 16


highest = lax.Precision.HIGHEST


def partner(value, axis, apart):
    mask = 2**apart
    pairs = [(source, source ^ mask) for source in range(lax.axis_size(axis))]
    return lax.ppermute(value, axis, pairs)


def rate_logs():
    ranks = jnp.arange(RATES).astype(jnp.float32)
    return -0.0001 * jnp.power(jnp.float32(500.0), ranks / (RATES - 1))


def decay_parts(logrates, flags):
    length = flags.shape[0]
    sums = jnp.cumsum(logrates, axis=1)
    segment = jnp.cumsum(flags)
    order = jnp.arange(length)
    inside = (segment[:, None] == segment[None, :]) & (order[:, None] >= order[None, :])
    spread = sums[:, :, None] - sums[:, None, :]
    lower_mat = jnp.where(inside[None], jnp.exp(jnp.where(inside[None], spread, 0.0)), 0.0)
    cumulative = jnp.where((segment == 0)[None, :], jnp.exp(sums), 0.0)
    end_weight = lower_mat[:, length - 1, :]
    return (lower_mat, cumulative, end_weight)


def join_pairs(earlier, later):
    return (earlier[0] * later[0], later[0][:, None, None] * earlier[1] + later[1])


def pick_pair(flag, first, second):
    return (jnp.where(flag, first[0], second[0]), jnp.where(flag, first[1], second[1]))


def combine_levels(state, from_higher, bits):
    position = lax.axis_index("seq")
    prefix, total = state
    for bit in bits:
        other = partner(total, "seq", bit)
        high_half = position // (1 << bit) % 2 == 1
        takes_other = jnp.logical_not(high_half) if from_higher else high_half
        prefix = pick_pair(takes_other, join_pairs(other, prefix), prefix)
        total = pick_pair(takes_other, join_pairs(other, total), join_pairs(total, other))
    return prefix, total


def identity_pair(heads, shape):
    return (jnp.ones((heads,), jnp.float32), jnp.zeros((heads,) + shape, jnp.float32))


def chain_kernel(bits, shift, a_ref, es_ref, eg_ref, fes_ref, feg_ref, pa_ref, pes_ref, peg_ref, tot_a, tot_e, recv_a, recv_e, sib_e, start_a, start_e, zero_a, zero_e, send_sem, recv_sem):
    e_refs, pe_refs, full_refs = (es_ref, eg_ref), (pes_ref, peg_ref), (fes_ref, feg_ref)
    seq_pos, dp_pos = lax.axis_index("seq"), lax.axis_index("dp")
    levels = len(bits)
    chains, groups = len(e_refs), start_a.shape[0]
    highs, partners = [], []
    for bit in bits:
        mask = 1 << bit
        up = seq_pos // mask % 2
        highs.append(up == 1)
        partners.append((dp_pos, seq_pos + mask - 2 * mask * up))
    core = seq_pos % 2
    sibling = (dp_pos, seq_pos + 1 - 2 * core)
    barrier = pltpu.get_barrier_semaphore()
    for device in partners + [sibling]:
        pl.semaphore_signal(barrier, inc=1, device_id=device, device_id_type=MESH)
    pl.semaphore_wait(barrier, levels + 1)
    base = levels * groups * (chains + 1)
    first = [(a_ref, zero_a)] + [(e_refs[c], zero_e.at[c]) for c in range(chains)]
    opening = []
    for k, (source, target) in enumerate(first):
        copy = pltpu.make_async_remote_copy(
            src_ref=source,
            dst_ref=target,
            send_sem=send_sem.at[base + chains + k],
            recv_sem=recv_sem.at[base + chains + k],
            device_id=sibling,
            device_id_type=MESH,
        )
        copy.start()
        opening.append(copy)
    pa_ref[...] = jnp.ones(pa_ref.shape, jnp.float32)
    for pe_ref in pe_refs:
        pe_ref[...] = jnp.zeros(pe_ref.shape, jnp.float32)
    for copy in opening:
        copy.wait()
    on_top = core == 1
    takes_first = (on_top, jnp.logical_not(on_top))
    own_a, other_a = a_ref[core], zero_a[core]
    start_a[...] = own_a * other_a
    for c in range(chains):
        own_e, other_e = e_refs[c][core], zero_e[c, core]
        start_e[c] = jnp.where(takes_first[c], own_a * other_e + own_e, other_a * own_e + other_e)
    for slot in range(levels + shift * (groups - 1)):
        active = [(g, slot - shift * g) for g in range(groups) if 0 <= slot - shift * g < levels]
        work = []
        for g, lev in active:
            src_a = start_a.at[g] if lev == 0 else tot_a.at[(lev - 1) % 2, g]
            src_e = [start_e.at[c, g] if lev == 0 else tot_e.at[(lev - 1) % 2, c, g] for c in range(chains)]
            if lev == levels - 1:
                needed = highs[lev].astype(jnp.int32)
                source = tot_e.at[(lev - 1) % 2, needed, g]
                pairs = [(source, recv_e.at[lev, 0, g])]
            else:
                pairs = [(src_a, recv_a.at[lev, g])] + [(src_e[c], recv_e.at[lev, c, g]) for c in range(chains)]
            copies = []
            for k, (source, target) in enumerate(pairs):
                index = (lev * groups + g) * (chains + 1) + k
                copy = pltpu.make_async_remote_copy(
                    src_ref=source,
                    dst_ref=target,
                    send_sem=send_sem.at[index],
                    recv_sem=recv_sem.at[index],
                    device_id=partners[lev],
                    device_id_type=MESH,
                )
                copy.start()
                copies.append(copy)
            work.append((g, lev, src_a, src_e, copies))
        for g, lev, src_a, src_e, copies in work:
            for copy in copies:
                copy.wait()
            last = lev == levels - 1
            if not last:
                o_a = recv_a[lev, g]
                t_a = src_a[...]
                tot_a[lev % 2, g] = o_a * t_a
            for c in range(chains):
                takes = jnp.logical_not(highs[lev]) if c == 1 else highs[lev]
                o_e = recv_e[lev, 0 if last else c, g]
                p_a = pa_ref[c, g]
                p_e = pe_refs[c][g]
                pe_refs[c][g] = jnp.where(takes, p_a * o_e + p_e, p_e)
                if not last:
                    pa_ref[c, g] = jnp.where(takes, o_a * p_a, p_a)
                    t_e = src_e[c][...]
                    tot_e[lev % 2, c, g] = jnp.where(takes, t_a * o_e + t_e, o_a * t_e + o_e)
    finals = []
    for c in range(chains):
        copy = pltpu.make_async_remote_copy(
            src_ref=pe_refs[c],
            dst_ref=sib_e.at[c],
            send_sem=send_sem.at[base + c],
            recv_sem=recv_sem.at[base + c],
            device_id=sibling,
            device_id_type=MESH,
        )
        copy.start()
        finals.append(copy)
    for c in range(chains):
        full_refs[c][core] = pe_refs[c][...]
    for copy in finals:
        copy.wait()
    for c in range(chains):
        full_refs[c][1 - core] = sib_e[c]
        whole = full_refs[c][...]
        full_refs[c][...] = jnp.where(takes_first[c], zero_a[...] * whole + zero_e[c], whole)


def combine_chains(decay_total, owns):
    heads, state, width = owns[0].shape
    halves, groups = 2, 2
    quarter = heads // (halves * groups)
    rows = state * width // 128
    levels = lax.axis_size("seq").bit_length() - 1
    bits = tuple(range(1, levels))
    shift = (levels - 1) // 2
    a_in = jnp.broadcast_to(decay_total.reshape(halves, groups, quarter, 1, 1), (halves, groups, quarter, 1, 128))
    e_in = [own.reshape(halves, groups, quarter, rows, 128) for own in owns]
    chains = len(owns)
    copies = len(bits) * groups * (chains + 1) + 2 * chains + 1
    vmem = pl.BlockSpec(memory_space=pltpu.VMEM)
    full = pl.pallas_call(
        functools.partial(chain_kernel, bits, shift),
        out_shape=tuple(jax.ShapeDtypeStruct((halves, groups, quarter, rows, 128), jnp.float32) for _ in owns),
        in_specs=[vmem] * 3,
        out_specs=(vmem, vmem),
        scratch_shapes=[
            pltpu.VMEM((chains, groups, quarter, 1, 128), jnp.float32),
            pltpu.VMEM((groups, quarter, rows, 128), jnp.float32),
            pltpu.VMEM((groups, quarter, rows, 128), jnp.float32),
            pltpu.VMEM((2, groups, quarter, 1, 128), jnp.float32),
            pltpu.VMEM((2, chains, groups, quarter, rows, 128), jnp.float32),
            pltpu.VMEM((len(bits), groups, quarter, 1, 128), jnp.float32),
            pltpu.VMEM((len(bits), chains, groups, quarter, rows, 128), jnp.float32),
            pltpu.VMEM((chains, groups, quarter, rows, 128), jnp.float32),
            pltpu.VMEM((groups, quarter, 1, 128), jnp.float32),
            pltpu.VMEM((chains, groups, quarter, rows, 128), jnp.float32),
            pltpu.VMEM((halves, groups, quarter, 1, 128), jnp.float32),
            pltpu.VMEM((chains, halves, groups, quarter, rows, 128), jnp.float32),
            pltpu.SemaphoreType.DMA((copies,)),
            pltpu.SemaphoreType.DMA((copies,)),
        ],
        compiler_params=pltpu.CompilerParams(collective_id=1, has_side_effects=True),
    )(a_in, *e_in)
    return [part.reshape(heads, state, width) for part in full]


def flat_bit_order(seq_bits, bits, near):
    order = []
    for b in near + list(range(bits)):
        if b < bits and b not in order:
            order.append(b)
    return order


def halving_kernel(seq_bits, orders, scale, *refs):
    lanes = len(orders)
    steps = len(orders[0])
    bufs, final_ref, scratch = refs[:lanes], refs[lanes], refs[lanes + 1:]
    small = sum(1 for step in range(steps) if (2 ** (steps - 1 - step)) % 8)
    per_lane = steps + steps + small
    send_sem, recv_sem = scratch[lanes * per_lane], scratch[lanes * per_lane + 1]
    seq_pos, dp_pos = lax.axis_index("seq"), lax.axis_index("dp")
    targets = {}
    for bit in range(steps):
        if bit < seq_bits:
            mask = 1 << bit
            mine = seq_pos // mask % 2
            targets[bit] = (mine, (dp_pos, seq_pos + mask - 2 * mask * mine))
        else:
            mask = 1 << (bit - seq_bits)
            mine = dp_pos // mask % 2
            targets[bit] = (mine, (dp_pos + mask - 2 * mask * mine, seq_pos))
    barrier = pltpu.get_barrier_semaphore()
    for bit in range(steps):
        pl.semaphore_signal(barrier, inc=1, device_id=targets[bit][1], device_id_type=MESH)
    pl.semaphore_wait(barrier, steps)
    currents = list(bufs)
    for step in range(steps):
        pending = []
        for lane in range(lanes):
            base = scratch[lane * per_lane:(lane + 1) * per_lane]
            recvs, accs, stages = base[:steps], base[steps:2 * steps], base[2 * steps:]
            mine, device = targets[orders[lane][step]]
            current = currents[lane]
            half = recvs[step].shape[0]
            if half % 8 == 0:
                source = current.at[pl.ds(pl.multiple_of((1 - mine) * half, 8), half)]
            else:
                source = stages[step - (steps - small)]
                source[...] = jnp.where(mine == 1, current[0:half], current[half:2 * half])
            copy = pltpu.make_async_remote_copy(
                src_ref=source,
                dst_ref=recvs[step],
                send_sem=send_sem.at[lane * steps + step],
                recv_sem=recv_sem.at[lane * steps + step],
                device_id=device,
                device_id_type=MESH,
            )
            copy.start()
            pending.append((lane, copy, mine, half, current, recvs[step], accs[step]))
        for lane, copy, mine, half, current, received, acc in pending:
            if half % 8 == 0:
                keep = current[pl.ds(pl.multiple_of(mine * half, 8), half)]
            else:
                keep = jnp.where(mine == 1, current[half:2 * half], current[0:half])
            copy.wait()
            acc[...] = keep + received[...]
            currents[lane] = acc
    rows, width = final_ref.shape[0], final_ref.shape[1] // lanes
    for lane in range(lanes):
        for row in range(rows):
            final_ref[row:row + 1, lane * width:(lane + 1) * width] = currents[lane][0:1, row * width:(row + 1) * width] * scale


def scatter_sum(product, scale):
    dp_size, seq_size = lax.axis_size("dp"), lax.axis_size("seq")
    seq_bits = seq_size.bit_length() - 1
    bits = seq_bits + dp_size.bit_length() - 1
    rows, cols = product.shape
    block = rows // (dp_size * seq_size)
    s = seq_bits
    orders = [
        flat_bit_order(s, bits, [0, 1, 3, s + 1, 2, 4, s + 2, s, s + 3]),
        flat_bit_order(s, bits, [0, 3, s + 1, 1, 4, s + 2, 2, s, s + 3]),
    ]
    lanes = len(orders)
    width = cols // lanes
    bufs = []
    for lane, order in enumerate(orders):
        part = product[:, lane * width:(lane + 1) * width].reshape(2**bits, block * width)
        source = [sum(((p >> (bits - 1 - i)) & 1) << b for i, b in enumerate(order)) for p in range(2**bits)]
        part = jnp.take(part, jnp.asarray(source, jnp.int32), axis=0)
        bufs.append(part)
    sizes = [2 ** (bits - 1 - step) for step in range(bits)]
    scratch = []
    for lane in range(lanes):
        scratch += [pltpu.VMEM((size, block * width), jnp.float32) for size in sizes]
        scratch += [pltpu.VMEM((size, block * width), jnp.float32) for size in sizes]
        scratch += [pltpu.VMEM((size, block * width), jnp.float32) for size in sizes if size % 8]
    scratch += [pltpu.SemaphoreType.DMA((lanes * bits,)), pltpu.SemaphoreType.DMA((lanes * bits,))]
    vmem = pl.BlockSpec(memory_space=pltpu.VMEM)
    return pl.pallas_call(
        functools.partial(halving_kernel, seq_bits, orders, scale),
        out_shape=jax.ShapeDtypeStruct((block, cols), jnp.float32),
        in_specs=[vmem] * lanes,
        out_specs=vmem,
        scratch_shapes=scratch,
        compiler_params=pltpu.CompilerParams(collective_id=0, has_side_effects=True),
    )(*bufs)


def local(normed, values, cotangent, w_bc, rate_index, starts):
    hidden = normed[0]
    length = hidden.shape[0]
    heads = rate_index.shape[1]
    width = values.shape[2]
    head_dim = width // heads
    state = w_bc.shape[1] // 2
    proj = jnp.dot(hidden, w_bc, preferred_element_type=jnp.float32).astype(jnp.bfloat16)
    bmat = proj[:, :state].astype(jnp.float32)
    cmat = proj[:, state:].astype(jnp.float32)
    levels_table = rate_logs()
    matches = rate_index[0][:, :, None] == jnp.arange(RATES)[None, None, :]
    logrates = jnp.sum(jnp.where(matches, levels_table[None, None, :], 0.0), axis=2)
    lower_mat, cumulative, end_weight = decay_parts(logrates, starts[0])
    vals = values[0].astype(jnp.float32).reshape(length, heads, head_dim)
    cots = cotangent[0].astype(jnp.float32).reshape(length, heads, head_dim)
    decay_total = cumulative[:, -1]
    ends = jnp.einsum("hk,kn,khp->hpn", end_weight, bmat, vals, precision=highest)
    feeds = jnp.einsum("hk,kn,khp->hpn", cumulative, cmat, cots, precision=highest)
    before, after = combine_chains(decay_total, [ends, feeds])
    scores = jnp.dot(cmat, bmat.T, precision=highest)
    mixed = lower_mat * scores[None]
    grad_vals = jnp.einsum("hts,thp->shp", mixed, cots, precision=highest)
    grad_vals = grad_vals + end_weight.T[:, :, None] * jnp.einsum(
        "sn,hpn->shp", bmat, after, precision=highest
    )
    paired = lower_mat * jnp.einsum("thp,shp->hts", cots, vals, precision=highest)
    grad_b = jnp.einsum("hts,tn->sn", paired, cmat, precision=highest)
    grad_b = grad_b + jnp.einsum("hs,shp,hpn->sn", end_weight, vals, after, precision=highest)
    grad_c = jnp.einsum("hts,sn->tn", paired, bmat, precision=highest)
    grad_c = grad_c + jnp.einsum("ht,thp,hpn->tn", cumulative, cots, before, precision=highest)
    grad_values = grad_vals.reshape(length, width).astype(jnp.bfloat16)[None]
    grad_bc = jnp.concatenate([grad_b, grad_c], axis=1).astype(jnp.bfloat16)
    scale = 1.0 / (lax.axis_size("dp") * lax.axis_size("seq") * length)
    product = lax.dot_general(
        hidden, grad_bc, (((0,), (0,)), ((), ())), preferred_element_type=jnp.float32
    )
    grad_wbc = scatter_sum(product, scale)
    return (grad_values, grad_wbc)


def solution(mesh):
    placed = (
        P("dp", "seq", None),
        P("dp", "seq", None),
        P("dp", "seq", None),
        P(),
        P("dp", None, "seq"),
        P("dp", "seq"),
    )
    return jax.shard_map(
        local,
        mesh=mesh,
        in_specs=placed,
        out_specs=(P("dp", "seq", None), P(("dp", "seq"), None)),
        check_vma=False,
    )
```
